512 devices in a mesh: row: 32 (over x, z_lo, core), col: 16 (over y, z_hi).
Axes of the slice: x: 4, y: 4, z: 16 (z_hi: 4, z_lo: 4; z = z_hi * 4 + z_lo), core: 2. Of those that a mesh axis runs over, the one named last changes fastest.
Arguments:
- hidden_img: bfloat16 [16384, 2432], P('row', 'col'), may hold values from -75 to 75
- hidden_txt: bfloat16 [3072, 2432], P('row', 'col'), may hold values from -75 to 75
- text_len: int32 [16], replicated, may hold values from 1 to 154, as said below
- step_index: int32 [16], replicated, may hold values from 0 to 27
- latent: float32 [16384, 64], P('row'), may hold values from -6 to 6
- cond: float32 [16, 2432], P(None, 'row'), may hold values from -6 to 6
- mod_weight: bfloat16 [2432, 7, 2432], P('row', None, 'col'), may hold values from -0.125 to 0.125
- qkv_weight: bfloat16 [2432, 3, 2048], P('row', None, 'col'), may hold values from -0.125 to 0.125
- kv_text_weight: bfloat16 [2432, 2, 2048], P('row', None, 'col'), may hold values from -0.125 to 0.125
- q_gain: float32 [64], replicated, may hold values from 0.5 to 6
- k_gain: float32 [2, 64], replicated, may hold values from 0.5 to 6
- out_weight: bfloat16 [2048, 2432], P('row', 'col'), may hold values from -6 to 6
- final_weight: bfloat16 [2432, 64], P('row'), may hold values from -0.125 to 0.125
Outputs:
- velocity: float32 [16384, 64], P('row')
- latent_next: float32 [16384, 64], P('row')
The draws below stay inside these ranges and needn't reach their ends.
Inputs may be any that keep to these rules, and one draw needn't show every extreme that they name: `text_len`: some request has exactly 154 text tokens in every draw.
All inputs are finite; a program needn't handle non-finite values.
Results may differ from the reference program's by a relative error of at most 0.015.
The reference program's roundings to bfloat16 on the way count: a program that leaves them out, or rounds other values in their place, can miss the bound.
Values may be sent and summed in bfloat16 or wider, within the bound.
A program may use at most 64 MiB of HBM per device.

```python
import jax
import jax.numpy as jnp
from jax import lax

D = 2432
HEAD_DIM = 64
HEADS = 32
PATCH_OUT = 64
TXT_MAX = 154
STEPS = 28
REQ = 16
IMG = 1024
TXT = 192
QKW = 2048


def scaled_rows(key, row_total, col_total):
    key_noise, key_cols, key_rows = jax.random.split(key, 3)
    ramp = 3.0 ** (jnp.arange(col_total, dtype=jnp.float32) / (col_total - 1) - 0.5)
    col_scale = ramp * jnp.exp(jax.random.uniform(key_cols, (col_total,), jnp.float32, jnp.log(0.5), jnp.log(2.0)))
    row_scale = jnp.exp(jax.random.uniform(key_rows, (row_total, 1), jnp.float32, jnp.log(0.5), jnp.log(5.0)))
    noise = jax.random.truncated_normal(key_noise, -4.0, 4.0, (row_total, col_total), jnp.float32)
    return (noise * col_scale * row_scale).astype(jnp.bfloat16)


def draw_hidden_img(key, part):
    return scaled_rows(jax.random.fold_in(key, 11), REQ * IMG, D)


def draw_hidden_txt(key, part):
    return scaled_rows(jax.random.fold_in(key, 12), REQ * TXT, D)


def draw_text_len(key, part):
    key_lens, key_pick = jax.random.split(jax.random.fold_in(key, 13))
    lengths = jax.random.randint(key_lens, (REQ,), 1, TXT_MAX + 1, dtype=jnp.int32)
    picked = jax.random.randint(key_pick, (), 0, REQ, dtype=jnp.int32)
    return lengths.at[picked].set(TXT_MAX)


def gain_values(key, shape, low, high):
    return jnp.exp(jax.random.uniform(key, shape, jnp.float32, jnp.log(low), jnp.log(high)))


def draw_q_gain(key, part):
    return gain_values(jax.random.fold_in(key, 14), (HEAD_DIM,), 0.5, 2.0)


def draw_k_gain(key, part):
    image_gain = gain_values(jax.random.fold_in(key, 15), (1, HEAD_DIM), 0.5, 2.0)
    text_gain = gain_values(jax.random.fold_in(key, 16), (1, HEAD_DIM), 1.5, 3.0)
    return jnp.concatenate([image_gain, text_gain], axis=0)


def plant(result, rng, low, high):
    place = [jax.random.randint(jax.random.fold_in(rng, axis), (), 0, length) for axis, length in enumerate(result.shape)]
    widest = result.shape.index(max(result.shape))
    neighbour = place[:widest] + [(place[widest] + 1) % result.shape[widest]] + place[widest + 1:]
    return result.at[tuple(place)].set(low).at[tuple(neighbour)].set(high)


def level_of(stream_key, shape, cuts, least, top_value):
    def one(axis_at, shards_of):
        steps = jax.random.uniform(jax.random.fold_in(jax.random.fold_in(stream_key, 6), axis_at), (shards_of,), jnp.float32, least / len(cuts), top_value / len(cuts))
        return jnp.repeat(jnp.exp(steps), shape[axis_at] // shards_of).reshape((-1,) + (1,) * (len(shape) - axis_at - 1))

    gain = one(*cuts[0])
    for cut in cuts[1:]:
        gain = gain * one(*cut)
    return gain


def normal_values(stream_key, dims, width, reach, cuts=(), kind=jnp.bfloat16):
    level = level_of(stream_key, dims, cuts, -0.22, 0.18) if cuts else 1.0
    entries = jax.random.normal(stream_key, dims, jnp.float32) * width * level
    return jnp.minimum(jnp.maximum(entries, -reach), reach).astype(kind)


def setup_inputs(seed: int = 0) -> dict:
    key_list = jax.random.split(jax.random.key(seed), 14)
    hidden_img = draw_hidden_img(jax.random.fold_in(key_list[13], 71), 0)
    hidden_txt = draw_hidden_txt(jax.random.fold_in(key_list[13], 71), 0)
    text_len = draw_text_len(jax.random.fold_in(key_list[13], 71), 0)
    step_index = plant(jax.random.randint(key_list[3], (REQ,), 0, STEPS), jax.random.fold_in(key_list[3], 1), 0, STEPS - 1).astype(jnp.int32)
    latent = normal_values(key_list[4], (REQ * IMG, PATCH_OUT), 1.0, 6.0, ((0, 32),), jnp.float32)
    cond = normal_values(key_list[5], (REQ, D), 1.0, 6.0, ((1, 32),), jnp.float32)
    mod_weight = normal_values(key_list[6], (D, 7, D), D ** -0.5, 0.125, ((0, 32), (2, 16)))
    qkv_weight = normal_values(key_list[7], (D, 3, QKW), D ** -0.5, 0.125, ((0, 32), (2, 16)))
    kv_text_weight = normal_values(key_list[8], (D, 2, QKW), D ** -0.5, 0.125, ((0, 32), (2, 16)))
    q_gain = draw_q_gain(jax.random.fold_in(key_list[13], 71), 0)
    k_gain = draw_k_gain(jax.random.fold_in(key_list[13], 71), 0)
    out_weight = normal_values(key_list[11], (QKW, D), (max(HEAD_DIM // 64, 1)) ** -0.5, 6.0, ((0, 32), (1, 16)))
    final_weight = normal_values(key_list[12], (D, PATCH_OUT), D ** -0.5, 0.125, ((0, 32),))
    return {"hidden_img": hidden_img, "hidden_txt": hidden_txt, "text_len": text_len, "step_index": step_index, "latent": latent, "cond": cond, "mod_weight": mod_weight, "qkv_weight": qkv_weight, "kv_text_weight": kv_text_weight, "q_gain": q_gain, "k_gain": k_gain, "out_weight": out_weight, "final_weight": final_weight}


EPS_NORM = 1e-06

def modulate_full(values, offset, stretch):
    average = lax.optimization_barrier(jnp.mean(values, axis=1, keepdims=True))
    mean_square = lax.optimization_barrier(jnp.mean(values * values, axis=1, keepdims=True))
    normed = (values - average) * lax.rsqrt(mean_square - average * average + EPS_NORM)
    return (normed * (1.0 + stretch) + offset).astype(jnp.bfloat16)

def head_norm(values, gain_row):
    mean_square = lax.optimization_barrier(jnp.mean(values * values, axis=-1, keepdims=True))
    return (values * lax.rsqrt(mean_square + EPS_NORM) * gain_row).astype(jnp.bfloat16)

def sigma_of(step_now):
    remain = 1.0 - step_now.astype(jnp.float32) / STEPS
    return 3.0 * remain / (1.0 + 2.0 * remain)

def reference(hidden_img, hidden_txt, text_len, step_index, latent, cond, mod_weight, qkv_weight, kv_text_weight, q_gain, k_gain, out_weight, final_weight):
    activated = jax.nn.silu(cond).astype(jnp.bfloat16)
    modulation = jnp.dot(activated, mod_weight.reshape(D, 7 * D), preferred_element_type=jnp.float32).reshape(REQ, 7, D)
    qkv_flat = qkv_weight.reshape(D, 3 * QKW)
    kv_flat = kv_text_weight.reshape(D, 2 * QKW)
    scaling = HEAD_DIM ** (-0.5)

    def one_request(operands):
        img_part, txt_part, length, mod_row, latent_part, step_now = operands
        img_ready = modulate_full(img_part.astype(jnp.float32), mod_row[0], mod_row[1])
        txt_ready = modulate_full(txt_part.astype(jnp.float32), mod_row[3], mod_row[4])
        img_proj = jnp.dot(img_ready, qkv_flat, preferred_element_type=jnp.float32).reshape(IMG, 3, HEADS, HEAD_DIM)
        txt_proj = jnp.dot(txt_ready, kv_flat, preferred_element_type=jnp.float32).reshape(TXT, 2, HEADS, HEAD_DIM)
        queries = head_norm(img_proj[:, 0], q_gain)
        all_keys = jnp.concatenate([head_norm(img_proj[:, 1], k_gain[0]), head_norm(txt_proj[:, 0], k_gain[1])], axis=0)
        all_values = jnp.concatenate([img_proj[:, 2].astype(jnp.bfloat16), txt_proj[:, 1].astype(jnp.bfloat16)], axis=0)
        key_valid = jnp.concatenate([jnp.ones((IMG,), dtype=bool), jnp.arange(TXT) < length])

        def attend(head_ops):
            q_head, k_head, v_head = head_ops
            scores = jnp.dot(q_head, k_head.T, preferred_element_type=jnp.float32) * scaling
            scores = jnp.where(key_valid[None, :], scores, -jnp.inf)
            row_max = lax.optimization_barrier(jnp.max(scores, axis=1, keepdims=True))
            weights = jnp.exp(scores - row_max)
            probabilities = (weights / lax.optimization_barrier(jnp.sum(weights, axis=1, keepdims=True))).astype(jnp.bfloat16)
            return jnp.dot(probabilities, v_head, preferred_element_type=jnp.float32).astype(jnp.bfloat16)
        attended = lax.map(attend, (jnp.moveaxis(queries, 1, 0), jnp.moveaxis(all_keys, 1, 0), jnp.moveaxis(all_values, 1, 0)))
        attended = jnp.moveaxis(attended, 0, 1).reshape(IMG, QKW)
        projected = jnp.dot(attended, out_weight, preferred_element_type=jnp.float32)
        updated = (img_part.astype(jnp.float32) + mod_row[2] * projected).astype(jnp.bfloat16)
        head_in = modulate_full(updated.astype(jnp.float32), mod_row[5], mod_row[6])
        velocity = jnp.dot(head_in, final_weight, preferred_element_type=jnp.float32)
        sigma_step = sigma_of(step_now + 1) - sigma_of(step_now)
        return (velocity, latent_part + sigma_step * velocity)
    velocity, latent_next = lax.map(one_request, (hidden_img.reshape(REQ, IMG, D), hidden_txt.reshape(REQ, TXT, D), text_len, modulation, latent.reshape(REQ, IMG, PATCH_OUT), step_index))
    return (velocity.reshape(REQ * IMG, PATCH_OUT), latent_next.reshape(REQ * IMG, PATCH_OUT))
```

```python
import jax
import jax.numpy as jnp
from jax import lax
from jax.experimental import pallas as pl
from jax.experimental.pallas import tpu as pltpu
from jax.sharding import PartitionSpec as P

STEPS = 28
EPS_NORM = 1e-06
WIDTH = 2432
MESH = pl.DeviceIdType.MESH
BF = jnp.bfloat16
F32 = jnp.float32
ANY = pl.BlockSpec(memory_space=pl.ANY)
VMEM = pl.BlockSpec(memory_space=pltpu.VMEM)
SMEM = pl.BlockSpec(memory_space=pltpu.SMEM)


def place():
    r, c = lax.axis_index("row"), lax.axis_index("col")
    return r // 8, (r // 2) % 4, r % 2, c // 4, c % 4


def device(x, zl, core, y, zh):
    return ((x * 4 + zl) * 2 + core, y * 4 + zh)


def up(v, d, n=4):
    return lax.rem(v + d + n, n)


def meet(devices):
    barrier = pltpu.get_barrier_semaphore()
    for d in devices:
        pl.semaphore_signal(barrier, inc=1, device_id=d, device_id_type=MESH)
    pl.semaphore_wait(barrier, len(devices))


class Post:
    def __init__(self, send_sem, recv_sem):
        self.send_sem, self.recv_sem, self.n, self.sent = send_sem, recv_sem, 0, []

    def send(self, src, dst, to, got):
        k = self.n
        self.n += 1
        copy = pltpu.make_async_remote_copy(
            src_ref=src, dst_ref=dst, send_sem=self.send_sem.at[k], recv_sem=self.recv_sem.at[k],
            device_id=to, device_id_type=MESH)
        copy.start()
        self.sent.append(copy)
        back = pltpu.make_async_remote_copy(
            src_ref=got, dst_ref=got, send_sem=self.send_sem.at[k], recv_sem=self.recv_sem.at[k],
            device_id=to, device_id_type=MESH)
        return back.wait_recv

    def finish(self):
        for copy in self.sent:
            copy.wait_send()


def gather_kernel(x_in, w_in, ow_in, mp, X, W, OW, M, part, tot, send_sem, recv_sem, own_sem):
    x, zl, core, y, zh = place()
    me = x * 4 + zl
    zg = zh * 4 + zl

    def at_chip(q):
        return (q * 2 + core, y * 4 + zh)

    def at_x(d):
        return device(up(x, d), zl, core, y, zh)

    def at_y(d):
        return device(x, zl, core, up(y, d), zh)

    def at_zh(d):
        return device(x, zl, core, y, up(zh, d))

    def at_zl(d):
        return device(x, up(zl, d), core, y, zh)

    def at_z(d):
        z = up(zg, d, 16)
        return device(x, lax.rem(z, 4), core, y, z // 4)

    partner = device(x, zl, 1 - core, y, zh)
    meet([at_chip(up(me, d, 16)) for d in range(1, 16)] + [at_zh(d) for d in (1, 2, 3)]
         + [at_y(d) for d in (1, 2, 3)] + [at_z(1), at_z(-1), partner])
    post = Post(send_sem, recv_sem)
    local = [pltpu.make_async_copy(x_in, X.at[y, zh], own_sem.at[0]),
             pltpu.make_async_copy(w_in, W.at[core, x, zl], own_sem.at[1]),
             pltpu.make_async_copy(ow_in, OW.at[core, x, zg], own_sem.at[2])]

    mods = []
    for d in range(1, 16):
        q, p = up(me, d, 16), up(me, -d, 16)
        mods.append(post.send(mp.at[q], part.at[me], at_chip(q), part.at[p]))
    zp = post.send(x_in, X.at[y, zh], at_zh(1), X.at[y, up(zh, -1)])
    zm = post.send(x_in, X.at[y, zh], at_zh(-1), X.at[y, up(zh, 1)])
    low, high = pl.ds(0, 80), pl.ds(80, 80)

    def y_out(z, src=None):
        s = X.at[y, z] if src is None else src
        return (post.send(s, X.at[y, z], at_y(1), X.at[up(y, -1), z]),
                post.send(s, X.at[y, z], at_y(-1), X.at[up(y, 1), z]))

    def y_on(z, waits):
        waits[0]()
        a = X.at[up(y, -1), z, low]
        f = post.send(a, a, at_y(1), X.at[up(y, 2), z, low])
        waits[1]()
        b = X.at[up(y, 1), z, high]
        g = post.send(b, b, at_y(-1), X.at[up(y, 2), z, high])
        return f, g

    y0 = y_out(zh, x_in)
    w_z = [post.send(w_in, W.at[core, x, zl], at_zl(d), W.at[core, x, up(zl, -d)]) for d in (1, 2, 3)]

    def ring(s):
        if s < 8:
            a, b = up(zg, 1 - s, 16), up(zg, s - 1, 16)
            p = ow_in if s == 1 else OW.at[core, x, a]
            q = ow_in if s == 1 else OW.at[core, x, b]
            return (post.send(p, OW.at[core, x, a], at_z(1), OW.at[core, x, up(zg, -s, 16)]),
                    post.send(q, OW.at[core, x, b], at_z(-1), OW.at[core, x, up(zg, s, 16)]))
        t, u = pl.ds(0, 32), pl.ds(32, 32)
        a, b = OW.at[core, x, up(zg, -7, 16), t], OW.at[core, x, up(zg, 7, 16), u]
        return (post.send(a, a, at_z(1), OW.at[core, x, up(zg, 8, 16), t]),
                post.send(b, b, at_z(-1), OW.at[core, x, up(zg, 8, 16), u]))

    def ring_on(s, waits):
        waits[0]()
        waits[1]()
        return ring(s + 1) if s < 8 else None

    step = ring(1)
    for copy in local:
        copy.start()

    for wait in mods:
        wait()
    part[me] = mp[me]
    total = part[0]
    for i in range(1, 16):
        total = total + part[i]
    tot[core] = total
    tw = post.send(tot.at[core], tot.at[core], partner, tot.at[1 - core])
    step = ring_on(1, step)
    y0f = y_on(zh, y0)
    tw()
    M[y, zh] = tot[0] + tot[1]
    m_z = [post.send(M.at[y, zh], M.at[y, zh], at_zh(d), M.at[y, up(zh, -d)]) for d in (1, 2, 3)]
    local[1].wait()
    for wait in w_z:
        wait()

    def x_out(ref):
        s = ref.at[core, x]
        return (post.send(s, s, at_x(1), ref.at[core, up(x, -1)]),
                post.send(s, s, at_x(-1), ref.at[core, up(x, 1)]))

    def x_on(ref, waits, half):
        waits[0]()
        a = ref.at[core, up(x, -1), pl.ds(0, half)]
        f = post.send(a, a, at_x(1), ref.at[core, up(x, 2), pl.ds(0, half)])
        waits[1]()
        b = ref.at[core, up(x, 1), pl.ds(half, half)]
        g = post.send(b, b, at_x(-1), ref.at[core, up(x, 2), pl.ds(half, half)])
        return f, g

    def across(ref, d):
        s = ref.at[core, up(x, d)]
        return post.send(s, s, partner, ref.at[1 - core, up(x, d)])

    last = []
    w_x = x_out(W)
    last.append(across(W, 0))
    step = ring_on(2, step)
    for wait in m_z:
        wait()
    last += [post.send(M.at[y], M.at[y], at_y(d), M.at[up(y, -d)]) for d in (1, 2, 3)]
    zp()
    a = X.at[y, up(zh, -1), low]
    zpf = post.send(a, a, at_zh(1), X.at[y, up(zh, 2), low])
    y1 = y_out(up(zh, -1))
    zm()
    b = X.at[y, up(zh, 1), high]
    zmf = post.send(b, b, at_zh(-1), X.at[y, up(zh, 2), high])
    y2 = y_out(up(zh, 1))
    step = ring_on(3, step)
    w_xf = x_on(W, w_x, 2)
    last += [across(W, -1), across(W, 1)]
    step = ring_on(4, step)
    y1f = y_on(up(zh, -1), y1)
    y2f = y_on(up(zh, 1), y2)
    step = ring_on(5, step)
    zpf()
    zmf()
    y3 = y_out(up(zh, 2))
    step = ring_on(6, step)
    step = ring_on(7, step)
    w_xf[0]()
    w_xf[1]()
    last.append(across(W, 2))
    ring_on(8, step)
    local[2].wait()
    o_x = x_out(OW)
    last.append(across(OW, 0))
    y3f = y_on(up(zh, 2), y3)
    for waits in (y0f, y1f, y2f, y3f):
        waits[0]()
        waits[1]()
    o_xf = x_on(OW, o_x, 8)
    last += [across(OW, -1), across(OW, 1)]
    o_xf[0]()
    o_xf[1]()
    last.append(across(OW, 2))
    for wait in last:
        wait()
    local[0].wait()
    post.finish()


def tdot(a, b):
    return lax.dot_general(a, b, (((0,), (0,)), ((), ())), preferred_element_type=F32)


def attention_kernel(X, W, M, G, text_len, out, ready, KB, VB, send_sem, recv_sem):
    x, zl, core, y, zh = place()
    partner = device(x, zl, 1 - core, y, zh)
    meet([partner])
    post = Post(send_sem, recv_sem)

    def tally(c, carry):
        v = X[c].astype(F32)
        s, q = carry
        return s + v.reshape(20, 8, 640).sum(axis=0), q + (v * v).reshape(20, 8, 640).sum(axis=0)

    zero = jnp.zeros((8, 640), F32)
    s, q = lax.fori_loop(0, 16, tally, (zero, zero))
    mean = jnp.sum(s, axis=0, keepdims=True) / WIDTH
    square = jnp.sum(q, axis=0, keepdims=True) / WIDTH
    rs = lax.rsqrt(square - mean * mean + EPS_NORM)

    def make_ready(c, carry):
        v = (X[c].astype(F32) - mean) * rs
        m = M[c].T
        a = v[:, :512] * (1.0 + m[:160, 1:2]) + m[:160, 0:1]
        b = v[:, 512:] * (1.0 + m[:160, 4:5]) + m[:160, 3:4]
        r = jnp.concatenate([a, b], axis=1).astype(BF)
        ready[pl.ds(pl.multiple_of(80 * c, 16), 80)] = r[:80]
        ready[pl.ds(pl.multiple_of(1280 + 80 * c, 16), 80)] = r[80:]
        return carry

    lax.fori_loop(0, 16, make_ready, 0)

    def normed(u, g):
        square = jnp.mean(u * u, axis=0, keepdims=True)
        return u * lax.rsqrt(square + EPS_NORM) * g

    def two(u, g):
        return jnp.concatenate([normed(u[:64], g), normed(u[64:], g)], axis=0)

    kv = tdot(W[:, 128:384], ready[:, :512])
    tkv = tdot(W[:, 384:640], ready[:, 512:])
    KB[0, :512] = two(kv[:128], G[:, 1:2]).T.astype(BF)
    KB[0, 512:] = two(tkv[:128], G[:, 2:3]).T.astype(BF)
    VB[0, :, :512] = kv[128:].astype(BF)
    VB[0, :, 512:] = tkv[128:].astype(BF)
    waits = [post.send(KB.at[0], KB.at[1], partner, KB.at[1]),
             post.send(VB.at[0], VB.at[1], partner, VB.at[1])]
    qt = two(tdot(W[:, :128], ready[:, :512]), G[:, 0:1])
    head = lax.broadcasted_iota(jnp.int32, (128, 512), 0) // 64
    qz = [jnp.where(head == h, qt, 0.0).astype(BF) for h in range(2)]
    for wait in waits:
        wait()
    length = text_len[x * 4 + zl]
    slot = lax.broadcasted_iota(jnp.int32, (128, 256), 0)
    valid = [(slot < 96) & (slot + 96 * owner < length) for owner in (core, 1 - core)]
    for part in range(2):
        for h in range(2):
            t = qz[h][:, 256 * part:256 * part + 256]
            scores = []
            for j in range(2):
                sc = jnp.dot(KB[j], t, preferred_element_type=F32) * 0.125
                scores += [sc[:512], jnp.where(valid[j], sc[512:], -jnp.inf)]
            top = scores[0].max(axis=0, keepdims=True)
            for sc in scores[1:]:
                top = jnp.maximum(top, sc.max(axis=0, keepdims=True))
            e = [jnp.exp(sc - top) for sc in scores]
            total = sum(v.sum(axis=0, keepdims=True) for v in e)
            inv = 1.0 / total
            p = [(v * inv).astype(BF) for v in e]
            o = 0.0
            for j in range(2):
                o = o + jnp.dot(VB[j, 64 * h:64 * h + 64, :512], p[2 * j], preferred_element_type=F32)
                o = o + jnp.dot(VB[j, 64 * h:64 * h + 64, 512:], p[2 * j + 1], preferred_element_type=F32)
            out[h, :, 256 * part:256 * part + 256] = o.astype(BF)
    post.finish()


def tail_kernel(att, X, M, OW, out, A, H, acc, U, ST, VP, VZ, send_sem, recv_sem, own_sem):
    x, zl, core, y, zh = place()

    def at_y(d):
        return device(x, zl, core, up(y, d), zh)

    def at_zh(d):
        return device(x, zl, core, y, up(zh, d))

    meet([at_y(d) for d in (1, 2, 3)] + [at_zh(d) for d in (1, 2, 3)])
    post = Post(send_sem, recv_sem)

    def lanes(z):
        return pl.ds(pl.multiple_of(128 * z, 128), 128)

    waits = []
    for d in (1, 3, 2):
        t = up(zh, d)
        waits.append(post.send(att.at[:, :, lanes(t)], A.at[:, y, zh], at_zh(d), A.at[:, y, up(zh, -d)]))
    local = [pltpu.make_async_copy(att.at[:, :, lanes(zh)], A.at[:, y, zh], own_sem.at[0]),
             pltpu.make_async_copy(X.at[y, :, :, lanes(zh)], H, own_sem.at[1])]
    for copy in local:
        copy.start()
    local[0].wait()
    for wait in waits:
        wait()
    ys = [post.send(A.at[:, y], A.at[:, y], at_y(d), A.at[:, up(y, -d)]) for d in (1, 3, 2)]

    def project(yy, first):
        for z in range(4):
            t = 0.0
            for h in range(2):
                a = A[h, yy].reshape(256, 128)
                w = OW[h, yy, 4 * z:4 * z + 4].reshape(256, 256)
                t = t + tdot(a, w)
            acc[z] = t if first else acc[z] + t

    project(y, True)
    for wait, d in zip(ys, (1, 3, 2)):
        wait()
        project(up(y, -d), False)
    local[1].wait()
    s = q = jnp.zeros((8, 128), F32)
    for z in range(4):
        m = M[4 * y + z].T
        u = (H[z].astype(F32) + m[:160, 2:3] * acc[z].T[:160]).astype(BF)
        U[z] = u
        v = u.astype(F32).reshape(20, 8, 128)
        s = s + v.sum(axis=0)
        q = q + (v * v).sum(axis=0)
    ST[y, 0] = s
    ST[y, 1] = q
    waits = [post.send(ST.at[y], ST.at[y], at_y(d), ST.at[up(y, -d)]) for d in (1, 3, 2)]
    for wait in waits:
        wait()
    st = ST[0] + ST[1] + (ST[2] + ST[3])
    mean = jnp.sum(st[0], axis=0, keepdims=True) / WIDTH
    square = jnp.sum(st[1], axis=0, keepdims=True) / WIDTH
    rs = lax.rsqrt(square - mean * mean + EPS_NORM)
    vel = 0.0
    for z in range(4):
        m = M[4 * y + z].T
        hi = (((U[z].astype(F32) - mean) * rs) * (1.0 + m[:160, 6:7]) + m[:160, 5:6]).astype(BF)
        for h in range(2):
            f = OW[h, y, z][:, 160:240]
            vel = vel + jnp.dot(f, hi[80 * h:80 * h + 80], preferred_element_type=F32)
    VP[y] = vel
    waits = [post.send(VP.at[y], VP.at[y], at_y(d), VP.at[up(y, -d)]) for d in (1, 3, 2)]
    for wait in waits:
        wait()
    VZ[zh] = VP[0] + VP[1] + (VP[2] + VP[3])
    waits = [post.send(VZ.at[zh], VZ.at[zh], at_zh(d), VZ.at[up(zh, -d)]) for d in (1, 3, 2)]
    for wait in waits:
        wait()
    for z in range(4):
        out[:, 128 * z:128 * z + 128] = VZ[z]
    post.finish()


def params(n, mb=60):
    return pltpu.CompilerParams(collective_id=n, has_side_effects=True, vmem_limit_bytes=mb << 20)


def sigma_of(step_now):
    remain = 1.0 - step_now.astype(F32) / STEPS
    return 3.0 * remain / (1.0 + 2.0 * remain)


def dma(n):
    return pltpu.SemaphoreType.DMA((n,))


def split80(v, axis):
    shape = v.shape
    v = v.reshape(shape[:axis] + (2, 76) + shape[axis + 1:])
    pads = [(0, 0)] * v.ndim
    pads[axis + 1] = (0, 4)
    return jnp.pad(v, pads).reshape(shape[:axis] + (160,) + shape[axis + 1:])


def per_device(hidden_img, hidden_txt, text_len, step_index, latent, cond, mod_weight, qkv_weight,
               kv_text_weight, q_gain, k_gain, out_weight, final_weight):
    activated = jax.nn.silu(cond).astype(BF)
    terms = jnp.dot(activated, mod_weight.reshape(76, 7 * 152), preferred_element_type=F32)
    terms = jnp.pad(split80(terms.reshape(16, 7, 152), 2), ((0, 0), (0, 1), (0, 96)))
    both = jnp.concatenate([hidden_img, hidden_txt, jnp.zeros((32, 152), BF)], axis=0)
    x_in = split80(both.T, 0)
    w_in = jnp.concatenate([qkv_weight.reshape(76, 384), kv_text_weight.reshape(76, 256)], axis=1)
    w_in = jnp.pad(w_in, ((0, 4), (0, 0)))
    ow_in = jnp.concatenate([split80(out_weight, 1), jnp.pad(final_weight.T, ((0, 0), (0, 20)))], axis=1)
    gains = jnp.pad(jnp.stack([q_gain, k_gain[0], k_gain[1]], axis=1), ((0, 0), (0, 125)))
    X, W, OW, M = pl.pallas_call(
        gather_kernel,
        out_shape=(jax.ShapeDtypeStruct((4, 4, 160, 640), BF), jax.ShapeDtypeStruct((2, 4, 4, 80, 640), BF),
                   jax.ShapeDtypeStruct((2, 4, 16, 64, 256), BF), jax.ShapeDtypeStruct((4, 4, 8, 256), F32)),
        in_specs=[ANY, ANY, ANY, VMEM],
        out_specs=(ANY, ANY, ANY, VMEM),
        scratch_shapes=[pltpu.VMEM((16, 8, 256), F32), pltpu.VMEM((2, 8, 256), F32), dma(80), dma(80), dma(3)],
        compiler_params=params(0),
        name="gather",
    )(x_in, w_in, ow_in, terms)
    M = M.reshape(16, 8, 256)
    att = pl.pallas_call(
        attention_kernel,
        out_shape=jax.ShapeDtypeStruct((2, 64, 512), BF),
        in_specs=[VMEM, VMEM, VMEM, VMEM, SMEM],
        out_specs=VMEM,
        scratch_shapes=[pltpu.VMEM((2560, 640), BF), pltpu.VMEM((2, 640, 128), BF),
                        pltpu.VMEM((2, 128, 640), BF), dma(2), dma(2)],
        compiler_params=params(1),
        name="attention",
    )(X.reshape(16, 160, 640), W.reshape(2560, 640), M, gains, text_len)
    vel = pl.pallas_call(
        tail_kernel,
        out_shape=jax.ShapeDtypeStruct((64, 512), F32),
        in_specs=[ANY, ANY, VMEM, VMEM],
        out_specs=VMEM,
        scratch_shapes=[pltpu.VMEM((2, 4, 4, 64, 128), BF), pltpu.VMEM((4, 160, 128), BF),
                        pltpu.VMEM((4, 128, 256), F32), pltpu.VMEM((4, 160, 128), BF),
                        pltpu.VMEM((4, 2, 8, 128), F32), pltpu.VMEM((4, 64, 128), F32),
                        pltpu.VMEM((4, 64, 128), F32), dma(16), dma(16), dma(2)],
        compiler_params=params(2),
        name="tail",
    )(att, X, M, OW)
    velocity = vel.T
    step_now = lax.dynamic_index_in_dim(step_index, lax.axis_index("row") // 2, 0, keepdims=False)
    sigma_step = sigma_of(step_now + 1) - sigma_of(step_now)
    return velocity, latent + sigma_step * velocity


def solution(mesh):
    in_specs = (P("row", "col"), P("row", "col"), P(), P(), P("row", None), P(None, "row"),
                P("row", None, "col"), P("row", None, "col"), P("row", None, "col"), P(), P(),
                P("row", "col"), P("row", None))
    out_specs = (P("row", None), P("row", None))
    return jax.shard_map(per_device, mesh=mesh, in_specs=in_specs, out_specs=out_specs, check_vma=False)
```

```python
import jax
import jax.numpy as jnp
from jax import lax
from jax.experimental import pallas as pl
from jax.experimental.pallas import tpu as pltpu
from jax.sharding import PartitionSpec as P

STEPS = 28
EPS_NORM = 1e-06
WIDTH = 2432
MESH = pl.DeviceIdType.MESH
BF = jnp.bfloat16
F32 = jnp.float32
VMEM = pl.BlockSpec(memory_space=pltpu.VMEM)
SMEM = pl.BlockSpec(memory_space=pltpu.SMEM)


def place():
    r, c = lax.axis_index("row"), lax.axis_index("col")
    return r // 8, (r // 2) % 4, r % 2, c // 4, c % 4


def device(x, zl, core, y, zh):
    return ((x * 4 + zl) * 2 + core, y * 4 + zh)


def up(v, d, n=4):
    return lax.rem(v + d + n, n)


def meet(devices):
    barrier = pltpu.get_barrier_semaphore()
    for d in devices:
        pl.semaphore_signal(barrier, inc=1, device_id=d, device_id_type=MESH)
    pl.semaphore_wait(barrier, len(devices))


class Post:
    def __init__(self, send_sem, recv_sem):
        self.send_sem, self.recv_sem, self.n, self.sent = send_sem, recv_sem, 0, []

    def send(self, src, dst, to, got):
        k = self.n
        self.n += 1
        copy = pltpu.make_async_remote_copy(
            src_ref=src, dst_ref=dst, send_sem=self.send_sem.at[k], recv_sem=self.recv_sem.at[k],
            device_id=to, device_id_type=MESH)
        copy.start()
        self.sent.append(copy)
        back = pltpu.make_async_remote_copy(
            src_ref=got, dst_ref=got, send_sem=self.send_sem.at[k], recv_sem=self.recv_sem.at[k],
            device_id=to, device_id_type=MESH)
        return back.wait_recv

    def finish(self):
        for copy in self.sent:
            copy.wait_send()


def tdot(a, b):
    return lax.dot_general(a, b, (((0,), (0,)), ((), ())), preferred_element_type=F32)


def all_of(waits):
    for wait in waits:
        wait()


def block_kernel(h_in, t_in, qkv_in, kv_in, ow_in, fw_in, mw_in, cond, G, text_len, sigma, latent,
                 out, X, W, OW, FX, FW, mp, part, tot, M, W2, R, KB, VB, QC, AT, A, acc, U, ST, VP, VZ,
                 send_sem, recv_sem):
    x, zl, core, y, zh = place()
    me = x * 4 + zl
    zg = zh * 4 + zl

    def at_chip(q):
        return (q * 2 + core, y * 4 + zh)

    def at_x(d):
        return device(up(x, d), zl, core, y, zh)

    def at_y(d):
        return device(x, zl, core, up(y, d), zh)

    def at_zh(d):
        return device(x, zl, core, y, up(zh, d))

    def at_zl(d):
        return device(x, up(zl, d), core, y, zh)

    def at_z(d):
        z = up(zg, d, 16)
        return device(x, lax.rem(z, 4), core, y, z // 4)

    partner = device(x, zl, 1 - core, y, zh)
    X[y, zh, :, 0:512] = h_in[...]
    X[y, zh, :, 512:640] = jnp.concatenate([t_in[...], jnp.zeros((152, 32), BF)], axis=1)
    meet([at_chip(up(me, d, 16)) for d in range(1, 16)] + [at_zh(d) for d in (1, 2, 3)]
         + [at_y(d) for d in (1, 2, 3)] + [at_z(1), at_z(-1), partner])
    post = Post(send_sem, recv_sem)
    send = post.send
    lo, hi = pl.ds(0, 80), pl.ds(80, 72)

    def relay(a, to, got):
        return send(a, a, to, got)

    def z_out(ch):
        return (relay(X.at[y, zh, ch], at_zh(1), X.at[y, up(zh, -1), ch]),
                relay(X.at[y, zh, ch], at_zh(-1), X.at[y, up(zh, 1), ch]))

    class Rows:
        def __init__(self, z):
            self.z, self.got = z, {}

        def out(self, ch, name):
            z = self.z
            self.got[name] = (relay(X.at[y, z, ch], at_y(1), X.at[up(y, -1), z, ch]),
                              relay(X.at[y, z, ch], at_y(-1), X.at[up(y, 1), z, ch]))

        def on(self):
            z = self.z
            self.got["lo"][0]()
            f = relay(X.at[up(y, -1), z, lo], at_y(1), X.at[up(y, 2), z, lo])
            self.got["hi"][1]()
            g = relay(X.at[up(y, 1), z, hi], at_y(-1), X.at[up(y, 2), z, hi])
            self.rest = [self.got["hi"][0], self.got["lo"][1], f, g]

        def done(self):
            all_of(self.rest)

    zp_lo = relay(X.at[y, zh, lo], at_zh(1), X.at[y, up(zh, -1), lo])
    zm_hi = relay(X.at[y, zh, hi], at_zh(-1), X.at[y, up(zh, 1), hi])
    zp_hi = relay(X.at[y, zh, hi], at_zh(1), X.at[y, up(zh, -1), hi])
    zm_lo = relay(X.at[y, zh, lo], at_zh(-1), X.at[y, up(zh, 1), lo])
    rows = [Rows(zh), Rows(up(zh, -1)), Rows(up(zh, 1)), Rows(up(zh, 2))]
    rows[0].out(lo, "lo")
    rows[0].out(hi, "hi")

    c = cond[...]
    act = (c * jax.nn.sigmoid(c)).astype(BF)
    mp[...] = jnp.zeros_like(mp)
    for g in range(7):
        mp[:, g, 0:152] = lax.dot_general(act, mw_in[g], (((1,), (1,)), ((), ())), preferred_element_type=F32)
    mods = []
    for d in range(1, 16):
        q, p = up(me, d, 16), up(me, -d, 16)
        mods.append(send(mp.at[q], part.at[me], at_chip(q), part.at[p]))
    W[core, x, zl] = jnp.zeros((5, 80, 128), BF)
    W[core, x, zl, 0:3, 0:76] = qkv_in[...]
    W[core, x, zl, 3:5, 0:76] = kv_in[...]
    w_z = [relay(W.at[core, x, zl], at_zl(d), W.at[core, x, up(zl, -d)]) for d in (1, 3, 2)]
    FX[x] = jnp.concatenate([fw_in[...], jnp.zeros((64, 52), BF)], axis=1)
    f_x = [relay(FX.at[x], at_x(d), FX.at[up(x, -d)]) for d in (1, 3, 2)]
    o = ow_in[...]
    OW[core, x, zg, 0:64] = o[:, :128]
    OW[core, x, zg, 64:80] = jnp.concatenate(
        [o[16 * g:16 * g + 16, 128:152] for g in range(4)] + [jnp.zeros((16, 32), BF)], axis=1)

    part[me] = mp[me]
    all_of(mods)
    total = part[0]
    for i in range(1, 16):
        total = total + part[i]
    tot[core] = total
    tw = relay(tot.at[core], partner, tot.at[1 - core])
    rows[0].on()
    tw()
    M[y, zh] = tot[0] + tot[1]
    m_z = [relay(M.at[y, zh], at_zh(d), M.at[y, up(zh, -d)]) for d in (1, 3, 2)]
    all_of(f_x)
    FW[core, zl] = FX[y]
    f_z = [relay(FW.at[core, zl], at_zl(d), FW.at[core, up(zl, -d)]) for d in (1, 3, 2)]

    def x_out(ref):
        return (relay(ref.at[core, x], at_x(1), ref.at[core, up(x, -1)]),
                relay(ref.at[core, x], at_x(-1), ref.at[core, up(x, 1)]))

    def x_on(ref, waits, half):
        waits[0]()
        f = relay(ref.at[core, up(x, -1), pl.ds(0, half)], at_x(1), ref.at[core, up(x, 2), pl.ds(0, half)])
        waits[1]()
        g = relay(ref.at[core, up(x, 1), pl.ds(half, half)], at_x(-1), ref.at[core, up(x, 2), pl.ds(half, half)])
        return f, g

    def across(ref, d):
        return relay(ref.at[core, up(x, d)], partner, ref.at[1 - core, up(x, d)])

    zp_lo()
    zpf = relay(X.at[y, up(zh, -1), lo], at_zh(1), X.at[y, up(zh, 2), lo])
    rows[1].out(lo, "lo")
    zm_hi()
    zmf = relay(X.at[y, up(zh, 1), hi], at_zh(-1), X.at[y, up(zh, 2), hi])
    rows[2].out(hi, "hi")
    all_of(w_z)
    w_x = x_out(W)
    w_a = [across(W, 0)]
    all_of(m_z)
    m_y = [relay(M.at[y], at_y(d), M.at[up(y, -d)]) for d in (1, 3, 2)]
    zp_hi()
    rows[1].out(hi, "hi")
    zm_lo()
    rows[2].out(lo, "lo")
    rows[0].done()

    def tally(blocks, carry):
        s, q = carry
        for yy, zz in blocks:
            v = X[yy, zz].astype(F32)
            s = s + v.reshape(19, 8, 640).sum(axis=0)
            q = q + (v * v).reshape(19, 8, 640).sum(axis=0)
        return s, q

    def ys(z):
        return [(up(y, d), z) for d in range(4)]

    zero = jnp.zeros((8, 640), F32)
    stat = tally(ys(zh), (zero, zero))
    w_xf = x_on(W, w_x, 2)
    w_a += [across(W, -1), across(W, 1)]
    rows[1].on()
    rows[2].on()
    all_of(f_z)
    f_a = [relay(FW.at[core], partner, FW.at[1 - core])]
    zpf()
    rows[3].out(lo, "lo")
    zmf()
    rows[3].out(hi, "hi")

    def background():
        for s in range(1, 9):
            if s < 8:
                a, b = up(zg, 1 - s, 16), up(zg, s - 1, 16)
                step = (relay(OW.at[core, x, a], at_z(1), OW.at[core, x, up(zg, -s, 16)]),
                        relay(OW.at[core, x, b], at_z(-1), OW.at[core, x, up(zg, s, 16)]))
            else:
                t, u = pl.ds(0, 48), pl.ds(48, 32)
                e = up(zg, 8, 16)
                step = (relay(OW.at[core, x, up(zg, -7, 16), t], at_z(1), OW.at[core, x, e, t]),
                        relay(OW.at[core, x, up(zg, 7, 16), u], at_z(-1), OW.at[core, x, e, u]))
            yield
            all_of(step)
        o_x = x_out(OW)
        o_a = [across(OW, 0)]
        yield
        o_xf = x_on(OW, o_x, 8)
        o_a += [across(OW, -1), across(OW, 1)]
        yield
        all_of(o_xf)
        o_a.append(across(OW, 2))
        yield
        all_of(o_a)
        yield

    work = background()
    next(work)
    all_of(w_xf)
    w_a.append(across(W, 2))
    rows[1].done()
    rows[2].done()
    next(work)
    stat = tally(ys(up(zh, -1)) + ys(up(zh, 1)), stat)
    all_of(w_a)
    all_of(m_y)

    def join(i, carry):
        xx, ll = i // 4, lax.rem(i, 4)
        for g in range(5):
            a = W[0, xx, ll, g].astype(F32)
            b = W[1, xx, ll, g].astype(F32)
            w = jnp.concatenate([a[:76], b[:76], jnp.zeros((8, 128), F32)], axis=0)
            W2[pl.ds(pl.multiple_of(160 * i, 32), 160), 128 * g:128 * g + 128] = w.astype(BF)
        return carry

    lax.fori_loop(0, 16, join, 0)
    rows[3].on()
    next(work)
    rows[3].done()
    s, q = tally(ys(up(zh, 2)), stat)
    next(work)
    mean = jnp.sum(s, axis=0, keepdims=True) / WIDTH
    square = jnp.sum(q, axis=0, keepdims=True) / WIDTH
    rs = lax.rsqrt(square - mean * mean + EPS_NORM)

    def make_ready(i, carry):
        yy, zz = i // 4, lax.rem(i, 4)
        v = (X[yy, zz].astype(F32) - mean) * rs
        m = M[yy, zz].T
        a = v[:, :512] * (1.0 + m[:152, 1:2]) + m[:152, 0:1]
        b = v[:, 512:] * (1.0 + m[:152, 4:5]) + m[:152, 3:4]
        r = jnp.concatenate([jnp.concatenate([a, b], axis=1), jnp.zeros((8, 640), F32)], axis=0)
        R[pl.ds(pl.multiple_of(160 * i, 32), 160)] = r.astype(BF)
        return carry

    lax.fori_loop(0, 8, make_ready, 0)
    next(work)
    lax.fori_loop(8, 16, make_ready, 0)
    next(work)

    def normed(u, g):
        square = jnp.mean(u * u, axis=0, keepdims=True)
        return u * lax.rsqrt(square + EPS_NORM) * g

    def two(u, g):
        return jnp.concatenate([normed(u[:64], g), normed(u[64:], g)], axis=0)

    kv = tdot(W2[:, 128:384], R[:, :512])
    tkv = tdot(W2[:, 384:640], R[:, 512:])
    KB[0, :512] = two(kv[:128], G[:, 1:2]).T.astype(BF)
    KB[0, 512:] = two(tkv[:128], G[:, 2:3]).T.astype(BF)
    VB[0, :, :512] = kv[128:].astype(BF)
    VB[0, :, 512:] = tkv[128:].astype(BF)
    waits = [send(KB.at[0], KB.at[1], partner, KB.at[1]), send(VB.at[0], VB.at[1], partner, VB.at[1])]
    next(work)
    qt = two(tdot(W2[:, :128], R[:, :512]), G[:, 0:1])
    head = lax.broadcasted_iota(jnp.int32, (128, 512), 0) // 64
    qz = [jnp.where(head == h, qt, 0.0).astype(BF) for h in range(2)]
    for t in range(4):
        QC[t] = jnp.concatenate([qz[0][:, 128 * t:128 * t + 128], qz[1][:, 128 * t:128 * t + 128]], axis=1)
    next(work)
    all_of(waits)

    length = text_len[me]
    slot = lax.broadcasted_iota(jnp.int32, (128, 256), 0)
    valid = [(slot < 96) & (slot + 96 * owner < length) for owner in (core, 1 - core)]
    a_z = {}
    for d in (2, 1, 3, 0):
        t = QC[up(zh, d)]
        scores = []
        for j in range(2):
            sc = jnp.dot(KB[j], t, preferred_element_type=F32) * 0.125
            scores += [sc[:512], jnp.where(valid[j], sc[512:], -jnp.inf)]
        top = scores[0].max(axis=0, keepdims=True)
        for sc in scores[1:]:
            top = jnp.maximum(top, sc.max(axis=0, keepdims=True))
        e = [jnp.exp(sc - top) for sc in scores]
        total = sum(v.sum(axis=0, keepdims=True) for v in e)
        inv = 1.0 / total
        p = [(v * inv).astype(BF) for v in e]
        o = 0.0
        for j in range(2):
            o = o + jnp.dot(VB[j, :, :512], p[2 * j], preferred_element_type=F32)
            o = o + jnp.dot(VB[j, :, 512:], p[2 * j + 1], preferred_element_type=F32)
        if d:
            AT[d - 1, 0] = o[:64, :128].astype(BF)
            AT[d - 1, 1] = o[64:, 128:].astype(BF)
            a_z[d] = send(AT.at[d - 1], A.at[:, y, zh], at_zh(d), A.at[:, y, up(zh, -d)])
        else:
            A[0, y, zh] = o[:64, :128].astype(BF)
            A[1, y, zh] = o[64:, 128:].astype(BF)
        next(work)

    a_y = []

    def along_y(z):
        for e in (1, 3, 2):
            a_y.append(relay(A.at[:, y, z], at_y(e), A.at[:, up(y, -e), z]))

    along_y(zh)
    for d in (1, 3, 2):
        a_z[d]()
        along_y(up(zh, -d))
    for _ in work:
        pass

    def project(yy, first):
        for z in range(4):
            t = 0.0
            for h in range(2):
                a = A[h, yy].reshape(256, 128)
                w = OW[h, yy, 4 * z:4 * z + 4]
                tail = jnp.concatenate([w[:, 64:80, 24 * g:24 * g + 24] for g in range(4)], axis=1)
                w = jnp.concatenate([w[:, :64], tail], axis=2).reshape(256, 152)
                t = t + tdot(a, w)
            acc[z] = t if first else acc[z] + t

    project(y, True)
    for k, e in enumerate((1, 3, 2)):
        all_of(a_y[k::3])
        project(up(y, -e), False)
    s = q = jnp.zeros((8, 128), F32)
    mine = pl.ds(pl.multiple_of(128 * zh, 128), 128)
    for z in range(4):
        m = M[y, z].T
        u = (X[y, z, :, mine].astype(F32) + m[:152, 2:3] * acc[z].T).astype(BF)
        U[z] = u
        v = u.astype(F32)
        s = s + v.reshape(19, 8, 128).sum(axis=0)
        q = q + (v * v).reshape(19, 8, 128).sum(axis=0)
    ST[y, 0] = s
    ST[y, 1] = q
    all_of([relay(ST.at[y], at_y(d), ST.at[up(y, -d)]) for d in (1, 3, 2)])
    all_of(f_a)
    st = ST[0] + ST[1] + (ST[2] + ST[3])
    mean = jnp.sum(st[0], axis=0, keepdims=True) / WIDTH
    square = jnp.sum(st[1], axis=0, keepdims=True) / WIDTH
    rs = lax.rsqrt(square - mean * mean + EPS_NORM)
    vel = 0.0
    for z in range(4):
        m = M[y, z].T
        head_in = ((U[z].astype(F32) - mean) * rs) * (1.0 + m[:152, 6:7]) + m[:152, 5:6]
        for h in range(2):
            vel = vel + jnp.dot(FW[h, z][:, :76], head_in[76 * h:76 * h + 76].astype(BF),
                                preferred_element_type=F32)
    VP[y] = vel
    all_of([relay(VP.at[y], at_y(d), VP.at[up(y, -d)]) for d in (1, 3, 2)])
    VZ[zh] = VP[0] + VP[1] + (VP[2] + VP[3])
    all_of([relay(VZ.at[zh], at_zh(d), VZ.at[up(zh, -d)]) for d in (1, 3, 2)])
    step = sigma[me]
    for z in range(4):
        v = VZ[z]
        out[0, :, 128 * z:128 * z + 128] = v
        out[1, :, 128 * z:128 * z + 128] = latent[:, 128 * z:128 * z + 128] + step * v
    post.finish()


def sigma_of(step_now):
    remain = 1.0 - step_now.astype(F32) / STEPS
    return 3.0 * remain / (1.0 + 2.0 * remain)


def dma(n):
    return pltpu.SemaphoreType.DMA((n,))


SCRATCH = [
    ((4, 4, 152, 640), BF),
    ((2, 4, 4, 5, 80, 128), BF),
    ((2, 4, 16, 80, 128), BF),
    ((4, 64, 128), BF),
    ((2, 4, 64, 128), BF),
    ((16, 8, 256), F32),
    ((16, 8, 256), F32),
    ((2, 8, 256), F32),
    ((4, 4, 8, 256), F32),
    ((2560, 640), BF),
    ((2560, 640), BF),
    ((2, 640, 128), BF),
    ((2, 128, 640), BF),
    ((4, 128, 256), BF),
    ((3, 2, 64, 128), BF),
    ((2, 4, 4, 64, 128), BF),
    ((4, 128, 152), F32),
    ((4, 152, 128), BF),
    ((4, 2, 8, 128), F32),
    ((4, 64, 128), F32),
    ((4, 64, 128), F32),
]


def per_device(hidden_img, hidden_txt, text_len, step_index, latent, cond, mod_weight, qkv_weight,
               kv_text_weight, q_gain, k_gain, out_weight, final_weight):
    gains = jnp.stack([q_gain, k_gain[0], k_gain[1]], axis=1)
    sigma = sigma_of(step_index + 1) - sigma_of(step_index)
    out = pl.pallas_call(
        block_kernel,
        out_shape=jax.ShapeDtypeStruct((2, 64, 512), F32),
        in_specs=[VMEM] * 9 + [SMEM, SMEM, VMEM],
        out_specs=VMEM,
        scratch_shapes=[pltpu.VMEM(s, t) for s, t in SCRATCH] + [dma(160), dma(160)],
        compiler_params=pltpu.CompilerParams(collective_id=0, has_side_effects=True, vmem_limit_bytes=60 << 20),
        name="block",
    )(hidden_img.T, hidden_txt.T, qkv_weight.transpose(1, 0, 2), kv_text_weight.transpose(1, 0, 2), out_weight,
      final_weight.T, mod_weight.transpose(1, 2, 0), cond, gains, text_len, sigma, latent.T)
    return out[0].T, out[1].T


def solution(mesh):
    in_specs = (P("row", "col"), P("row", "col"), P(), P(), P("row", None), P(None, "row"),
                P("row", None, "col"), P("row", None, "col"), P("row", None, "col"), P(), P(),
                P("row", "col"), P("row", None))
    out_specs = (P("row", None), P("row", None))
    return jax.shard_map(per_device, mesh=mesh, in_specs=in_specs, out_specs=out_specs, check_vma=False)
```

```python
import jax
import jax.numpy as jnp
from jax import lax
from jax.experimental import pallas as pl
from jax.experimental.pallas import tpu as pltpu
from jax.sharding import PartitionSpec as P

STEPS = 28
EPS_NORM = 1e-06
WIDTH = 2432
MESH = pl.DeviceIdType.MESH
BF = jnp.bfloat16
F32 = jnp.float32
VMEM = pl.BlockSpec(memory_space=pltpu.VMEM)
SMEM = pl.BlockSpec(memory_space=pltpu.SMEM)


def place():
    r, c = lax.axis_index("row"), lax.axis_index("col")
    return r // 8, (r // 2) % 4, r % 2, c // 4, c % 4


def device(x, zl, core, y, zh):
    return ((x * 4 + zl) * 2 + core, y * 4 + zh)


def up(v, d, n=4):
    return lax.rem(v + d + n, n)


def sigma_of(step_now):
    remain = 1.0 - step_now.astype(F32) / STEPS
    return 3.0 * remain / (1.0 + 2.0 * remain)


class Post:
    def __init__(self, send_sem, recv_sem):
        self.send_sem, self.recv_sem, self.n, self.sent, self.todo = send_sem, recv_sem, 0, [], []

    def send(self, src, dst, to, got):
        k = self.n
        self.n += 1
        copy = pltpu.make_async_remote_copy(
            src_ref=src, dst_ref=dst, send_sem=self.send_sem.at[k], recv_sem=self.recv_sem.at[k],
            device_id=to, device_id_type=MESH)
        copy.start()
        self.sent.append(copy)
        back = pltpu.make_async_remote_copy(
            src_ref=got, dst_ref=got, send_sem=self.send_sem.at[k], recv_sem=self.recv_sem.at[k],
            device_id=to, device_id_type=MESH)
        todo = [True]
        self.todo.append((todo, back.wait_recv))

        def wait():
            assert todo[0]
            todo[0] = False
            back.wait_recv()
        return wait

    def finish(self):
        for copy in self.sent:
            copy.wait_send()


def drain(post):
    for todo, wait in post.todo:
        if todo[0]:
            wait()
    post.finish()


def tdot(a, b):
    return lax.dot_general(a, b, (((0,), (0,)), ((), ())), preferred_element_type=F32)


def all_of(waits):
    for wait in waits:
        wait()


def block_kernel(h_in, t_in, qkv_in, kv_in, ow_in, fw_in, mw_in, cond, qg, kg, text_len, step_index, latent,
                 out, X, W, OW, FX, FW, SS, mp, mx, ms, ml, tot, M, W2, R, PI, PT, KB, VB, QC, AT, A, acc, U, ST, VP, VZ,
                 send_sem, recv_sem):
    x, zl, core, y, zh = place()
    me = x * 4 + zl

    def at_x(d):
        return device(up(x, d), zl, core, y, zh)

    def at_y(d):
        return device(x, zl, core, up(y, d), zh)

    def at_zh(d):
        return device(x, zl, core, y, up(zh, d))

    def at_zl(d):
        return device(x, up(zl, d), core, y, zh)

    partner = device(x, zl, 1 - core, y, zh)
    three = (1, 3, 2)
    peers = [f(d) for f in (at_x, at_y, at_zh, at_zl) for d in three] + [partner]
    barrier = pltpu.get_barrier_semaphore()
    for p in peers:
        pl.semaphore_signal(barrier, inc=1, device_id=p, device_id_type=MESH)

    own = jnp.concatenate([h_in[...], jnp.concatenate([t_in[...], jnp.zeros((152, 32), BF)], axis=1)], axis=1)
    X[y, zh] = own
    v = own.astype(F32)
    SS[y, zh] = jnp.concatenate([jnp.sum(v, axis=0, keepdims=True), jnp.sum(v * v, axis=0, keepdims=True)], axis=0)
    W[core, x, zl] = jnp.zeros((5, 80, 128), BF)
    W[core, x, zl, 0:3, 0:76] = qkv_in[...]
    W[core, x, zl, 3:5, 0:76] = kv_in[...]
    FX[x] = jnp.concatenate([fw_in[...], jnp.zeros((64, 52), BF)], axis=1)
    o = ow_in[...]
    OW[core, x, zh, zl, 0:64] = o[:, :128]
    OW[core, x, zh, zl, 64:80] = jnp.concatenate(
        [o[16 * g:16 * g + 16, 128:152] for g in range(4)] + [jnp.zeros((16, 32), BF)], axis=1)
    mp[...] = jnp.zeros_like(mp)
    pl.semaphore_wait(barrier, len(peers))

    post = Post(send_sem, recv_sem)
    send = post.send
    lo, hi = pl.ds(0, 80), pl.ds(80, 72)

    def relay(a, to, got):
        return send(a, a, to, got)

    class Rows:
        def __init__(self, z):
            self.z, self.got = z, {}

        def out(self, ch, name):
            z = self.z
            self.got[name] = (relay(X.at[y, z, ch], at_y(1), X.at[up(y, -1), z, ch]),
                              relay(X.at[y, z, ch], at_y(-1), X.at[up(y, 1), z, ch]))

        def on(self):
            z = self.z
            self.got["lo"][0]()
            f = relay(X.at[up(y, -1), z, lo], at_y(1), X.at[up(y, 2), z, lo])
            self.got["hi"][1]()
            g = relay(X.at[up(y, 1), z, hi], at_y(-1), X.at[up(y, 2), z, hi])
            self.rest = [self.got["hi"][0], self.got["lo"][1], f, g]

        def done(self):
            all_of(self.rest)

    rows = [Rows(zh), Rows(up(zh, -1)), Rows(up(zh, 1)), Rows(up(zh, 2))]
    ss_z = [relay(SS.at[y, zh], at_zh(d), SS.at[y, up(zh, -d)]) for d in three]
    rows[0].out(lo, "lo")
    rows[0].out(hi, "hi")
    w_z = [relay(W.at[core, x, zl], at_zl(d), W.at[core, x, up(zl, -d)]) for d in three]
    zp_lo = relay(X.at[y, zh, lo], at_zh(1), X.at[y, up(zh, -1), lo])
    zm_hi = relay(X.at[y, zh, hi], at_zh(-1), X.at[y, up(zh, 1), hi])

    c = cond[...]
    act = (c * jax.nn.sigmoid(c)).astype(BF)
    for g in range(7):
        t = lax.dot_general(act, mw_in[g], (((1,), (1,)), ((), ())), preferred_element_type=F32)
        for i in range(4):
            mp[i, :, g, 0:152] = t[4 * i:4 * i + 4]
    mods = [send(mp.at[up(x, d)], mx.at[x], at_x(d), mx.at[up(x, -d)]) for d in three]
    f_x = [relay(FX.at[x], at_x(d), FX.at[up(x, -d)]) for d in three]
    mx[x] = mp[x]
    all_of(mods)
    ms[...] = (mx[0] + mx[1]) + (mx[2] + mx[3])
    mods = [send(ms.at[up(zl, d)], ml.at[zl], at_zl(d), ml.at[up(zl, -d)]) for d in three]
    zp_hi = relay(X.at[y, zh, hi], at_zh(1), X.at[y, up(zh, -1), hi])
    zm_lo = relay(X.at[y, zh, lo], at_zh(-1), X.at[y, up(zh, 1), lo])
    all_of(ss_z)
    ss_y = [relay(SS.at[y], at_y(d), SS.at[up(y, -d)]) for d in three]
    ml[zl] = ms[zl]

    def x_out(part):
        a = part(x)
        return relay(a, at_x(1), part(up(x, -1))), relay(a, at_x(-1), part(up(x, 1)))

    def x_on(part, waits):
        waits[0]()
        t, u = pl.ds(0, 2), pl.ds(2, 2)
        f = relay(part(up(x, -1)).at[t], at_x(1), part(up(x, 2)).at[t])
        waits[1]()
        g = relay(part(up(x, 1)).at[u], at_x(-1), part(up(x, 2)).at[u])
        return f, g

    def w_part(i):
        return W.at[core, i]

    def across(d):
        return relay(W.at[core, up(x, d)], partner, W.at[1 - core, up(x, d)])

    rows[0].on()
    all_of(w_z)
    w_x = x_out(w_part)
    w_a = [across(0)]
    zp_lo()
    rows[1].out(lo, "lo")
    zm_hi()
    rows[2].out(hi, "hi")
    all_of(mods)
    tot[core] = (ml[0] + ml[1]) + (ml[2] + ml[3])
    tw = relay(tot.at[core], partner, tot.at[1 - core])
    all_of(ss_y)
    s = jnp.zeros((2, 640), F32)
    for i in range(16):
        s = s + SS[i // 4, i % 4]
    s = s / WIDTH
    mean = s[0:1]
    rs = lax.rsqrt(s[1:2] - mean * mean + EPS_NORM)
    tw()
    M[y, zh] = tot[0] + tot[1]
    m_z = [relay(M.at[y, zh], at_zh(d), M.at[y, up(zh, -d)]) for d in three]
    zpf = relay(X.at[y, up(zh, -1), lo], at_zh(1), X.at[y, up(zh, 2), lo])
    zmf = relay(X.at[y, up(zh, 1), hi], at_zh(-1), X.at[y, up(zh, 2), hi])
    all_of(f_x)
    FW[core, zl] = FX[y]
    o_l = [relay(OW.at[core, x, zh, zl], at_zl(d), OW.at[core, x, zh, up(zl, -d)]) for d in three]
    f_z = [relay(FW.at[core, zl], at_zl(d), FW.at[core, up(zl, -d)]) for d in three]
    w_xf = x_on(w_part, w_x)
    w_a += [across(-1), across(1)]
    zp_hi()
    rows[1].out(hi, "hi")
    zm_lo()
    rows[2].out(lo, "lo")
    rows[0].done()
    all_of(w_xf)
    w_a.append(across(2))
    rows[1].on()
    rows[2].on()
    all_of(w_a)
    all_of(m_z)
    m_y = [relay(M.at[y], at_y(d), M.at[up(y, -d)]) for d in three]

    def join(i, carry):
        xx, ll = lax.rem(i, 4), up(zh, i // 4)
        for g in range(5):
            a = W[0, xx, ll, g].astype(F32)
            b = W[1, xx, ll, g].astype(F32)
            w = jnp.concatenate([a[:76], b[:76], jnp.zeros((8, 128), F32)], axis=0)
            W2[pl.ds(pl.multiple_of(160 * i, 32), 160), 128 * g:128 * g + 128] = w.astype(BF)
        return carry

    lax.fori_loop(0, 16, join, 0)
    all_of(m_y)

    def ready(k):
        def one(i, carry):
            yy, zz = i, up(zh, k)
            v = (X[yy, zz].astype(F32) - mean) * rs
            m = M[yy, zz].T
            a = v[:, :512] * (1.0 + m[:152, 1:2]) + m[:152, 0:1]
            b = v[:, 512:] * (1.0 + m[:152, 4:5]) + m[:152, 3:4]
            r = jnp.concatenate([jnp.concatenate([a, b], axis=1), jnp.zeros((8, 640), F32)], axis=0)
            R[pl.ds(pl.multiple_of(640 * k + 160 * i, 32), 160)] = r.astype(BF)
            return carry

        lax.fori_loop(0, 4, one, 0)

    def dots(k, a, b, image):
        n = 640 * k
        lanes = slice(0, 512) if image else slice(512, 640)
        return tdot(W2[n:n + 640, a:b], R[n:n + 640, lanes])

    ready(0)
    PI[...] = dots(0, 0, 384, True)
    PT[...] = dots(0, 384, 640, False)
    zpf()
    rows[3].out(lo, "lo")
    zmf()
    rows[3].out(hi, "hi")

    def o_part(d):
        return lambda i: OW.at[core, i, up(zh, d)]

    def o_across(d):
        z = up(zh, d)
        return relay(OW.at[core, :, z], partner, OW.at[1 - core, :, z])

    def background():
        all_of(o_l)
        a, t, u = OW.at[core, x], pl.ds(0, 2), pl.ds(2, 2)
        zp = relay(a.at[zh], at_zh(1), a.at[up(zh, -1)])
        zm = relay(a.at[zh], at_zh(-1), a.at[up(zh, 1)])
        x0 = x_out(o_part(0))
        yield
        x0 = x_on(o_part(0), x0)
        yield
        zp()
        zpf = relay(a.at[up(zh, -1), t], at_zh(1), a.at[up(zh, 2), t])
        x3 = x_out(o_part(-1))
        zm()
        zmf = relay(a.at[up(zh, 1), u], at_zh(-1), a.at[up(zh, 2), u])
        x1 = x_out(o_part(1))
        all_of(x0)
        last = [o_across(0)]
        yield
        x3 = x_on(o_part(-1), x3)
        x1 = x_on(o_part(1), x1)
        yield
        zpf()
        zmf()
        x2 = x_out(o_part(2))
        all_of(x3)
        last.append(o_across(-1))
        all_of(x1)
        last.append(o_across(1))
        yield
        x2 = x_on(o_part(2), x2)
        yield
        all_of(x2)
        last.append(o_across(2))
        yield
        all_of(last)
        yield

    work = background()
    all_of(f_z)
    f_a = [relay(FW.at[core], partner, FW.at[1 - core])]
    next(work)
    rows[1].done()
    ready(3)
    PI[...] += dots(3, 0, 384, True)
    PT[...] += dots(3, 384, 640, False)
    rows[2].done()
    ready(1)
    PI[...] += dots(1, 0, 384, True)
    PT[...] += dots(1, 384, 640, False)
    rows[3].on()
    next(work)
    rows[3].done()
    ready(2)

    def normed(u, g):
        square = jnp.mean(u * u, axis=0, keepdims=True)
        return u * lax.rsqrt(square + EPS_NORM) * g

    def two(u, g):
        return jnp.concatenate([normed(u[:64], g), normed(u[64:], g)], axis=0)

    G = jnp.concatenate([qg[...], kg[...], jnp.zeros((5, 64), F32)], axis=0)
    G = jnp.concatenate([G, G], axis=1).T[:64]
    kv = PI[128:384] + dots(2, 128, 384, True)
    tkv = PT[...] + dots(2, 384, 640, False)
    KB[0, :512] = two(kv[:128], G[:, 1:2]).T.astype(BF)
    KB[0, 512:] = two(tkv[:128], G[:, 2:3]).T.astype(BF)
    VB[0, :, :512] = kv[128:].astype(BF)
    VB[0, :, 512:] = tkv[128:].astype(BF)
    waits = [send(KB.at[0], KB.at[1], partner, KB.at[1]), send(VB.at[0], VB.at[1], partner, VB.at[1])]
    qt = two(PI[0:128] + dots(2, 0, 128, True), G[:, 0:1])
    head = lax.broadcasted_iota(jnp.int32, (128, 512), 0) // 64
    qz = [jnp.where(head == h, qt, 0.0).astype(BF) for h in range(2)]
    for t in range(4):
        QC[t] = jnp.concatenate([qz[0][:, 128 * t:128 * t + 128], qz[1][:, 128 * t:128 * t + 128]], axis=1)
    next(work)
    all_of(waits)

    length = text_len[me]
    slot = lax.broadcasted_iota(jnp.int32, (128, 256), 0)
    valid = [(slot < 96) & (slot + 96 * owner < length) for owner in (core, 1 - core)]
    a_z = {}
    for d in (2, 1, 3, 0):
        t = QC[up(zh, d)]
        scores = []
        for j in range(2):
            sc = jnp.dot(KB[j], t, preferred_element_type=F32) * 0.125
            scores += [sc[:512], jnp.where(valid[j], sc[512:], -jnp.inf)]
        top = scores[0].max(axis=0, keepdims=True)
        for sc in scores[1:]:
            top = jnp.maximum(top, sc.max(axis=0, keepdims=True))
        e = [jnp.exp(sc - top) for sc in scores]
        total = sum(v.sum(axis=0, keepdims=True) for v in e)
        inv = 1.0 / total
        p = [(v * inv).astype(BF) for v in e]
        o = 0.0
        for j in range(2):
            o = o + jnp.dot(VB[j, :, :512], p[2 * j], preferred_element_type=F32)
            o = o + jnp.dot(VB[j, :, 512:], p[2 * j + 1], preferred_element_type=F32)
        if d:
            AT[d - 1, 0] = o[:64, :128].astype(BF)
            AT[d - 1, 1] = o[64:, 128:].astype(BF)
            a_z[d] = send(AT.at[d - 1], A.at[:, y, zh], at_zh(d), A.at[:, y, up(zh, -d)])
        else:
            A[0, y, zh] = o[:64, :128].astype(BF)
            A[1, y, zh] = o[64:, 128:].astype(BF)
        next(work)

    a_y = []

    def along_y(z):
        for e in (1, 3, 2):
            a_y.append(relay(A.at[:, y, z], at_y(e), A.at[:, up(y, -e), z]))

    along_y(zh)
    for d in (1, 3, 2):
        a_z[d]()
        along_y(up(zh, -d))
    for _ in work:
        pass

    def project(yy, first):
        for z in range(4):
            t = 0.0
            for h in range(2):
                a = A[h, yy].reshape(256, 128)
                w = OW[h, yy, z]
                tail = jnp.concatenate([w[:, 64:80, 24 * g:24 * g + 24] for g in range(4)], axis=1)
                w = jnp.concatenate([w[:, :64], tail], axis=2).reshape(256, 152)
                t = t + tdot(a, w)
            acc[z] = t if first else acc[z] + t

    project(y, True)
    for k, e in enumerate((1, 3, 2)):
        all_of(a_y[k::3])
        project(up(y, -e), False)
    s = q = jnp.zeros((8, 128), F32)
    mine = pl.ds(pl.multiple_of(128 * zh, 128), 128)
    for z in range(4):
        m = M[y, z].T
        u = (X[y, z, :, mine].astype(F32) + m[:152, 2:3] * acc[z].T).astype(BF)
        U[z] = u
        v = u.astype(F32)
        s = s + v.reshape(19, 8, 128).sum(axis=0)
        q = q + (v * v).reshape(19, 8, 128).sum(axis=0)
    ST[y, 0] = s
    ST[y, 1] = q
    all_of([relay(ST.at[y], at_y(d), ST.at[up(y, -d)]) for d in (1, 3, 2)])
    all_of(f_a)
    st = ST[0] + ST[1] + (ST[2] + ST[3])
    mean = jnp.sum(st[0], axis=0, keepdims=True) / WIDTH
    square = jnp.sum(st[1], axis=0, keepdims=True) / WIDTH
    rs = lax.rsqrt(square - mean * mean + EPS_NORM)
    vel = 0.0
    for z in range(4):
        m = M[y, z].T
        head_in = ((U[z].astype(F32) - mean) * rs) * (1.0 + m[:152, 6:7]) + m[:152, 5:6]
        for h in range(2):
            vel = vel + jnp.dot(FW[h, z][:, :76], head_in[76 * h:76 * h + 76].astype(BF),
                                preferred_element_type=F32)
    VP[y] = vel
    all_of([relay(VP.at[y], at_y(d), VP.at[up(y, -d)]) for d in (1, 3, 2)])
    VZ[zh] = (VP[0] + VP[1] + (VP[2] + VP[3])).astype(BF)
    all_of([relay(VZ.at[zh], at_zh(d), VZ.at[up(zh, -d)]) for d in (1, 3, 2)])
    now = jnp.full((8, 128), step_index[me], jnp.int32)
    step = (sigma_of(now + 1) - sigma_of(now))[0:1]
    for z in range(4):
        v = VZ[z].astype(F32)
        out[0, :, 128 * z:128 * z + 128] = v
        out[1, :, 128 * z:128 * z + 128] = latent[:, 128 * z:128 * z + 128] + step * v
    post.finish()


def dma(n):
    return pltpu.SemaphoreType.DMA((n,))


SCRATCH = [
    ((4, 4, 152, 640), BF),
    ((2, 4, 4, 5, 80, 128), BF),
    ((2, 4, 4, 4, 80, 128), BF),
    ((4, 64, 128), BF),
    ((2, 4, 64, 128), BF),
    ((4, 4, 2, 640), F32),
    ((4, 4, 8, 256), F32),
    ((4, 4, 8, 256), F32),
    ((4, 8, 256), F32),
    ((4, 8, 256), F32),
    ((2, 8, 256), F32),
    ((4, 4, 8, 256), F32),
    ((2560, 640), BF),
    ((2560, 640), BF),
    ((384, 512), F32),
    ((256, 128), F32),
    ((2, 640, 128), BF),
    ((2, 128, 640), BF),
    ((4, 128, 256), BF),
    ((3, 2, 64, 128), BF),
    ((2, 4, 4, 64, 128), BF),
    ((4, 128, 152), F32),
    ((4, 152, 128), BF),
    ((4, 2, 8, 128), F32),
    ((4, 64, 128), F32),
    ((4, 64, 128), BF),
]


def per_device(hidden_img, hidden_txt, text_len, step_index, latent, cond, mod_weight, qkv_weight,
               kv_text_weight, q_gain, k_gain, out_weight, final_weight):
    out = pl.pallas_call(
        block_kernel,
        out_shape=jax.ShapeDtypeStruct((2, 64, 512), F32),
        in_specs=[VMEM] * 10 + [SMEM, SMEM, VMEM],
        out_specs=VMEM,
        scratch_shapes=[pltpu.VMEM(s, t) for s, t in SCRATCH] + [dma(160), dma(160)],
        compiler_params=pltpu.CompilerParams(collective_id=0, has_side_effects=True, vmem_limit_bytes=60 << 20),
        name="block",
    )(hidden_img.T, hidden_txt.T, qkv_weight.transpose(1, 0, 2), kv_text_weight.transpose(1, 0, 2), out_weight,
      final_weight.T, mod_weight.transpose(1, 2, 0), cond, q_gain.reshape(1, 64), k_gain, text_len, step_index, latent.T)
    return out[0].T, out[1].T


def solution(mesh):
    in_specs = (P("row", "col"), P("row", "col"), P(), P(), P("row", None), P(None, "row"),
                P("row", None, "col"), P("row", None, "col"), P("row", None, "col"), P(), P(),
                P("row", "col"), P("row", None))
    out_specs = (P("row", None), P("row", None))
    return jax.shard_map(per_device, mesh=mesh, in_specs=in_specs, out_specs=out_specs, check_vma=False)
```

```python
import jax
import jax.numpy as jnp
from jax import lax
from jax.experimental import pallas as pl
from jax.experimental.pallas import tpu as pltpu
from jax.sharding import PartitionSpec as P

STEPS = 28
EPS_NORM = 1e-06
WIDTH = 2432
MESH = pl.DeviceIdType.MESH
BF = jnp.bfloat16
F32 = jnp.float32
VMEM = pl.BlockSpec(memory_space=pltpu.VMEM)
SMEM = pl.BlockSpec(memory_space=pltpu.SMEM)


def place():
    r, c = lax.axis_index("row"), lax.axis_index("col")
    return r // 8, (r // 2) % 4, r % 2, c // 4, c % 4


def device(x, zl, core, y, zh):
    return ((x * 4 + zl) * 2 + core, y * 4 + zh)


def up(v, d, n=4):
    return lax.rem(v + d + n, n)


def sigma_of(step_now):
    remain = 1.0 - step_now.astype(F32) / STEPS
    return 3.0 * remain / (1.0 + 2.0 * remain)


class Post:
    def __init__(self, send_sem, recv_sem):
        self.send_sem, self.recv_sem, self.n, self.sent, self.todo = send_sem, recv_sem, 0, [], []

    def send(self, src, dst, to, got):
        k = self.n
        self.n += 1
        copy = pltpu.make_async_remote_copy(
            src_ref=src, dst_ref=dst, send_sem=self.send_sem.at[k], recv_sem=self.recv_sem.at[k],
            device_id=to, device_id_type=MESH)
        copy.start()
        self.sent.append(copy)
        back = pltpu.make_async_remote_copy(
            src_ref=got, dst_ref=got, send_sem=self.send_sem.at[k], recv_sem=self.recv_sem.at[k],
            device_id=to, device_id_type=MESH)
        todo = [True]
        self.todo.append((todo, back.wait_recv))

        def wait():
            assert todo[0]
            todo[0] = False
            back.wait_recv()
        return wait

    def finish(self):
        for copy in self.sent:
            copy.wait_send()


def drain(post):
    for todo, wait in post.todo:
        if todo[0]:
            wait()
    post.finish()


def tdot(a, b):
    return lax.dot_general(a, b, (((0,), (0,)), ((), ())), preferred_element_type=F32)


def all_of(waits):
    for wait in waits:
        wait()


def block_kernel(h_in, t_in, qkv_in, kv_in, ow_in, fw_in, mw_in, cond, qg, kg, text_len, step_index, latent,
                 out, X, W, OW, FX, FW, SS, mp, mx, ms, ml, tot, M, W2, R, PI, PT, KB, VB, QC, AT, A, acc, U, ST, VP, VZ,
                 send_sem, recv_sem):
    x, zl, core, y, zh = place()
    me = x * 4 + zl

    def at_x(d):
        return device(up(x, d), zl, core, y, zh)

    def at_y(d):
        return device(x, zl, core, up(y, d), zh)

    def at_zh(d):
        return device(x, zl, core, y, up(zh, d))

    def at_zl(d):
        return device(x, up(zl, d), core, y, zh)

    partner = device(x, zl, 1 - core, y, zh)
    three = (1, 3, 2)
    peers = [f(d) for f in (at_x, at_y, at_zl) for d in three] + [at_zh(1), at_zh(-1), partner]
    barrier = pltpu.get_barrier_semaphore()
    for p in peers:
        pl.semaphore_signal(barrier, inc=1, device_id=p, device_id_type=MESH)

    own = jnp.concatenate([h_in[...], jnp.concatenate([t_in[...], jnp.zeros((152, 32), BF)], axis=1)], axis=1)
    X[y, zh] = own
    v = own.astype(F32)
    SS[y, zh] = jnp.concatenate([jnp.sum(v, axis=0, keepdims=True), jnp.sum(v * v, axis=0, keepdims=True)], axis=0)
    W[core, x, zl] = jnp.zeros((5, 80, 128), BF)
    W[core, x, zl, 0:3, 0:76] = qkv_in[...]
    W[core, x, zl, 3:5, 0:76] = kv_in[...]
    FX[x] = jnp.concatenate([fw_in[...], jnp.zeros((64, 52), BF)], axis=1)
    o = ow_in[...]
    OW[core, x, zl, zh, 0:64] = o[:, :128]
    OW[core, x, zl, zh, 64:80] = jnp.concatenate(
        [o[16 * g:16 * g + 16, 128:152] for g in range(4)] + [jnp.zeros((16, 32), BF)], axis=1)
    mp[...] = jnp.zeros_like(mp)
    pl.semaphore_wait(barrier, len(peers))

    post = Post(send_sem, recv_sem)
    send = post.send
    lo, hi = pl.ds(0, 80), pl.ds(80, 72)

    def relay(a, to, got):
        return send(a, a, to, got)

    LO, HI = [(0, 80)], [(80, 72)]

    class Rows:
        def __init__(self, z):
            self.z, self.low, self.high, self.rest = z, [], [], []

        def out(self, chunks):
            for first, size in chunks:
                ch = pl.ds(first, size)
                a = X.at[y, self.z, ch]
                got = (relay(a, at_y(1), X.at[up(y, -1), self.z, ch]), relay(a, at_y(-1), X.at[up(y, 1), self.z, ch]))
                if first < 80:
                    self.low.append((got[0], ch))
                    self.rest.append(got[1])
                else:
                    self.high.append((got[1], ch))
                    self.rest.append(got[0])

        def on(self, which):
            for wait, ch in which:
                e = -1 if which is self.low else 1
                wait()
                a = X.at[up(y, e), self.z, ch]
                self.rest.append(relay(a, at_y(-e), X.at[up(y, 2), self.z, ch]))

        def done(self):
            all_of(self.rest)

    def along_z(buf, first=None):
        a = buf(zh)
        return relay(a, at_zh(1), buf(up(zh, -1))), relay(a, at_zh(-1), buf(up(zh, 1)))

    def on_z(buf, waits):
        all_of(waits)
        return relay(buf(up(zh, -1)), at_zh(1), buf(up(zh, 2)))

    def x_out(part):
        a = part(x)
        return relay(a, at_x(1), part(up(x, -1))), relay(a, at_x(-1), part(up(x, 1)))

    def x_on(part, waits, n):
        waits[0]()
        t, u = pl.ds(0, n[0]), pl.ds(n[0], n[1])
        f = relay(part(up(x, -1)).at[t], at_x(1), part(up(x, 2)).at[t])
        waits[1]()
        g = relay(part(up(x, 1)).at[u], at_x(-1), part(up(x, 2)).at[u])
        return f, g

    def w_part(d):
        return lambda i: W.at[core, i, up(zl, d)]

    def across(ref, d):
        return relay(ref.at[core, :, up(zl, d)], partner, ref.at[1 - core, :, up(zl, d)])

    rows = [Rows(zh), Rows(up(zh, -1)), Rows(up(zh, 1)), Rows(up(zh, 2))]
    ss_z = along_z(lambda z: SS.at[y, z])
    w_x0 = x_out(w_part(0))
    rows[0].out(LO + HI)
    C0, C1, C2, C3 = (0, 48), (48, 32), (80, 48), (128, 24)

    def z_up(c):
        ch = pl.ds(*c)
        return relay(X.at[y, zh, ch], at_zh(1), X.at[y, up(zh, -1), ch])

    def z_down(c):
        ch = pl.ds(*c)
        return relay(X.at[y, zh, ch], at_zh(-1), X.at[y, up(zh, 1), ch])

    def w_to(d):
        return relay(W.at[core, x, zl], at_zl(d), W.at[core, x, up(zl, -d)])

    zp_0, zm_2 = z_up(C0), z_down(C2)

    c = cond[...]
    act = (c * jax.nn.sigmoid(c)).astype(BF)
    for g in range(7):
        t = lax.dot_general(act, mw_in[g], (((1,), (1,)), ((), ())), preferred_element_type=F32)
        for i in range(4):
            mp[i, :, g, 0:152] = t[4 * i:4 * i + 4]
    mods = [send(mp.at[up(x, d)], mx.at[x], at_x(d), mx.at[up(x, -d)]) for d in three]
    f_x = [relay(FX.at[x], at_x(d), FX.at[up(x, -d)]) for d in three]
    mx[x] = mp[x]
    all_of(mods)
    ms[...] = (mx[0] + mx[1]) + (mx[2] + mx[3])
    mods = [send(ms.at[up(zl, d)], ml.at[zl], at_zl(d), ml.at[up(zl, -d)]) for d in three]
    zp_1, zm_3 = z_up(C1), z_down(C3)
    ml[zl] = ms[zl]
    w_x0 = x_on(w_part(0), w_x0, (3, 2))
    ss_f = on_z(lambda z: SS.at[y, z], ss_z)
    rows[0].on(rows[0].low)
    rows[0].on(rows[0].high)
    all_of(mods)
    tot[core] = (ml[0] + ml[1]) + (ml[2] + ml[3])
    tw = relay(tot.at[core], partner, tot.at[1 - core])
    tw()
    M[y, zh] = tot[0] + tot[1]
    m_z = along_z(lambda z: M.at[y, z])
    w_z = [w_to(1), w_to(3)]
    ss_f()
    ss_y = [relay(SS.at[y], at_y(d), SS.at[up(y, -d)]) for d in three]
    all_of(w_x0)
    w_a = [across(W, 0)]
    m_f = on_z(lambda z: M.at[y, z], m_z)
    w_z.append(w_to(2))
    zp_2, zm_1 = z_up(C2), z_down(C1)
    w_z[0]()
    w_x3 = x_out(w_part(-1))
    w_z[1]()
    w_x1 = x_out(w_part(1))
    zp_0()
    rows[1].out([C0])
    zm_2()
    rows[2].out([C2])
    zp_3, zm_0 = z_up(C3), z_down(C0)
    m_f()
    m_y = [relay(M.at[y], at_y(d), M.at[up(y, -d)]) for d in three]
    w_x3 = x_on(w_part(-1), w_x3, (3, 2))
    w_x1 = x_on(w_part(1), w_x1, (3, 2))
    all_of(f_x)
    FW[core, zl] = FX[y]
    zp_1()
    rows[1].out([C1])
    zm_3()
    rows[2].out([C3])
    zpf = []
    for c in (C0, C1):
        ch = pl.ds(*c)
        zpf.append(relay(X.at[y, up(zh, -1), ch], at_zh(1), X.at[y, up(zh, 2), ch]))
    for c in (C2, C3):
        ch = pl.ds(*c)
        zpf.append(relay(X.at[y, up(zh, 1), ch], at_zh(-1), X.at[y, up(zh, 2), ch]))
    w_z[2]()
    w_x2 = x_out(w_part(2))
    all_of(ss_y)
    s = jnp.zeros((2, 640), F32)
    for i in range(16):
        s = s + SS[i // 4, i % 4]
    s = s / WIDTH
    mean = s[0:1]
    rs = lax.rsqrt(s[1:2] - mean * mean + EPS_NORM)
    o_h = along_z(lambda z: OW.at[core, x, zl, z])
    all_of(w_x3)
    w_a.append(across(W, -1))
    all_of(w_x1)
    w_a.append(across(W, 1))
    w_x2 = x_on(w_part(2), w_x2, (3, 2))
    zp_2()
    rows[1].out([C2])
    zm_1()
    rows[2].out([C1])
    rows[1].on(rows[1].low)
    rows[2].on(rows[2].high)
    rows[0].done()
    zp_3()
    rows[1].out([C3])
    zm_0()
    rows[2].out([C0])
    f_z = [relay(FW.at[core, zl], at_zl(d), FW.at[core, up(zl, -d)]) for d in three]
    all_of(w_x2)
    w_a.append(across(W, 2))
    o_hf = on_z(lambda z: OW.at[core, x, zl, z], o_h)
    all_of(w_a)

    def join(i, carry):
        xx, ll = lax.rem(i, 4), up(zh, i // 4)
        for g in range(5):
            a = W[0, xx, ll, g].astype(F32)
            b = W[1, xx, ll, g].astype(F32)
            w = jnp.concatenate([a[:76], b[:76], jnp.zeros((8, 128), F32)], axis=0)
            W2[pl.ds(pl.multiple_of(160 * i, 32), 160), 128 * g:128 * g + 128] = w.astype(BF)
        return carry

    lax.fori_loop(0, 16, join, 0)
    rows[1].on(rows[1].high)
    rows[2].on(rows[2].low)
    o_hf()
    o_l = [relay(OW.at[core, x, zl], at_zl(d), OW.at[core, x, up(zl, -d)]) for d in three]

    def ready(k):
        def one(i, carry):
            yy, zz = i, up(zh, k)
            v = (X[yy, zz].astype(F32) - mean) * rs
            m = M[yy, zz].T
            a = v[:, :512] * (1.0 + m[:152, 1:2]) + m[:152, 0:1]
            b = v[:, 512:] * (1.0 + m[:152, 4:5]) + m[:152, 3:4]
            r = jnp.concatenate([jnp.concatenate([a, b], axis=1), jnp.zeros((8, 640), F32)], axis=0)
            R[pl.ds(pl.multiple_of(640 * k + 160 * i, 32), 160)] = r.astype(BF)
            return carry

        lax.fori_loop(0, 4, one, 0)

    def dots(k, a, b, image):
        n = 640 * k
        lanes = slice(0, 512) if image else slice(512, 640)
        return tdot(W2[n:n + 640, a:b], R[n:n + 640, lanes])

    def o_part(d):
        return lambda i: OW.at[core, i, up(zl, d)]

    def background():
        def fan(d):
            part = o_part(d)
            return [relay(part(x), at_x(e), part(up(x, -e))) for e in three]

        x0 = fan(0)
        yield
        o_l[0]()
        x3 = fan(-1)
        o_l[1]()
        x1 = fan(1)
        yield
        o_l[2]()
        x2 = fan(2)
        all_of(x0)
        last = [across(OW, 0)]
        yield
        yield
        all_of(x3)
        last.append(across(OW, -1))
        all_of(x1)
        last.append(across(OW, 1))
        yield
        yield
        all_of(x2)
        last.append(across(OW, 2))
        all_of(last)
        yield

    def add(k):
        ready(k)
        PI[...] += dots(k, 0, 384, True)
        PT[...] += dots(k, 384, 640, False)

    work = background()
    all_of(m_y)
    ready(0)
    PI[...] = dots(0, 0, 384, True)
    PT[...] = dots(0, 384, 640, False)
    zpf[0]()
    rows[3].out([C0])
    zpf[2]()
    rows[3].out([C2])
    next(work, None)
    rows[1].done()
    add(3)
    zpf[1]()
    rows[3].out([C1])
    zpf[3]()
    rows[3].out([C3])
    rows[2].done()
    add(1)
    rows[3].on(rows[3].low)
    rows[3].on(rows[3].high)
    all_of(f_z)
    f_a = [relay(FW.at[core], partner, FW.at[1 - core])]
    next(work, None)
    rows[3].done()
    ready(2)

    def normed(u, g):
        square = jnp.mean(u * u, axis=0, keepdims=True)
        return u * lax.rsqrt(square + EPS_NORM) * g

    def two(u, g):
        return jnp.concatenate([normed(u[:64], g), normed(u[64:], g)], axis=0)

    G = jnp.concatenate([qg[...], kg[...], jnp.zeros((5, 64), F32)], axis=0)
    G = jnp.concatenate([G, G], axis=1).T[:64]
    kv = PI[128:384] + dots(2, 128, 384, True)
    tkv = PT[...] + dots(2, 384, 640, False)
    KB[0, :512] = two(kv[:128], G[:, 1:2]).T.astype(BF)
    KB[0, 512:] = two(tkv[:128], G[:, 2:3]).T.astype(BF)
    VB[0, :128, :512] = kv[128:].astype(BF)
    VB[0, :128, 512:] = tkv[128:].astype(BF)
    VB[0, 128:] = jnp.ones((16, 640), BF)
    waits = [send(KB.at[0], KB.at[1], partner, KB.at[1]), send(VB.at[0], VB.at[1], partner, VB.at[1])]
    qt = two(PI[0:128] + dots(2, 0, 128, True), G[:, 0:1])
    head = lax.broadcasted_iota(jnp.int32, (128, 512), 0) // 64
    qz = [jnp.where(head == h, qt, 0.0).astype(BF) * 0.125 for h in range(2)]
    for t in range(4):
        QC[t] = jnp.concatenate([qz[0][:, 128 * t:128 * t + 128], qz[1][:, 128 * t:128 * t + 128]], axis=1)
    next(work, None)
    all_of(waits)

    length = text_len[me]
    slot = lax.broadcasted_iota(jnp.int32, (128, 256), 0)
    valid = [(slot < 96) & (slot + 96 * owner < length) for owner in (core, 1 - core)]
    a_z = {}
    for d in (2, 1, 3, 0):
        t = QC[up(zh, d)]
        scores = []
        for j in range(2):
            sc = jnp.dot(KB[j], t, preferred_element_type=F32)
            scores += [sc[:512], jnp.where(valid[j], sc[512:], -jnp.inf)]
        top = scores[0].max(axis=0, keepdims=True)
        for sc in scores[1:]:
            top = jnp.maximum(top, sc.max(axis=0, keepdims=True))
        p = [jnp.exp(sc - top).astype(BF) for sc in scores]
        o = 0.0
        for j in range(2):
            o = o + jnp.dot(VB[j, :, :512], p[2 * j], preferred_element_type=F32)
            o = o + jnp.dot(VB[j, :, 512:], p[2 * j + 1], preferred_element_type=F32)
        o = o[:128] / o[128:129]
        if d:
            AT[d - 1, 0] = o[:64, :128].astype(BF)
            AT[d - 1, 1] = o[64:, 128:].astype(BF)
            a_z[d] = send(AT.at[d - 1], A.at[:, y, zh], at_zh(d), A.at[:, y, up(zh, -d)])
        else:
            A[0, y, zh] = o[:64, :128].astype(BF)
            A[1, y, zh] = o[64:, 128:].astype(BF)
        next(work, None)

    a_y = []

    def along_y(z):
        for e in (1, 3, 2):
            a_y.append(relay(A.at[:, y, z], at_y(e), A.at[:, up(y, -e), z]))

    along_y(zh)
    for d in (1, 3, 2):
        a_z[d]()
        along_y(up(zh, -d))
    all_of(f_a)
    fw = [jnp.concatenate([FW[0, z][:, :76], FW[1, z][:, :76]], axis=1) for z in range(4)]
    for _ in work:
        pass

    def project(yy, first):
        for z in range(4):
            t = 0.0
            for h in range(2):
                a = A[h, yy].reshape(256, 128)
                w = OW[h, yy, :, z]
                tail = jnp.concatenate([w[:, 64:80, 24 * g:24 * g + 24] for g in range(4)], axis=1)
                w = jnp.concatenate([w[:, :64], tail], axis=2).reshape(256, 152)
                t = t + tdot(a, w)
            acc[z] = t if first else acc[z] + t

    project(y, True)
    for k, e in enumerate((1, 3, 2)):
        all_of(a_y[k::3])
        project(up(y, -e), False)
    s = q = jnp.zeros((8, 128), F32)
    mine = pl.ds(pl.multiple_of(128 * zh, 128), 128)
    for z in range(4):
        m = M[y, z].T
        u = (X[y, z, :, mine].astype(F32) + m[:152, 2:3] * acc[z].T).astype(BF)
        U[z] = u
        v = u.astype(F32)
        s = s + v.reshape(19, 8, 128).sum(axis=0)
        q = q + (v * v).reshape(19, 8, 128).sum(axis=0)
    ST[y, 0] = s
    ST[y, 1] = q
    all_of([relay(ST.at[y], at_y(d), ST.at[up(y, -d)]) for d in (1, 3, 2)])
    st = ST[0] + ST[1] + (ST[2] + ST[3])
    mean = jnp.sum(st[0], axis=0, keepdims=True) / WIDTH
    square = jnp.sum(st[1], axis=0, keepdims=True) / WIDTH
    rs = lax.rsqrt(square - mean * mean + EPS_NORM)
    vel = 0.0
    for z in range(4):
        m = M[y, z].T
        head_in = ((U[z].astype(F32) - mean) * rs) * (1.0 + m[:152, 6:7]) + m[:152, 5:6]
        vel = vel + jnp.dot(fw[z], head_in.astype(BF), preferred_element_type=F32)
    VP[y] = vel
    all_of([relay(VP.at[y], at_y(d), VP.at[up(y, -d)]) for d in (1, 3, 2)])
    VZ[zh] = (VP[0] + VP[1] + (VP[2] + VP[3])).astype(BF)
    all_of([relay(VZ.at[zh], at_zh(d), VZ.at[up(zh, -d)]) for d in (1, 3, 2)])
    now = jnp.full((8, 128), step_index[me], jnp.int32)
    step = (sigma_of(now + 1) - sigma_of(now))[0:1]
    for z in range(4):
        v = VZ[z].astype(F32)
        out[0, :, 128 * z:128 * z + 128] = v
        out[1, :, 128 * z:128 * z + 128] = latent[:, 128 * z:128 * z + 128] + step * v
    post.finish()


def dma(n):
    return pltpu.SemaphoreType.DMA((n,))


SCRATCH = [
    ((4, 4, 152, 640), BF),
    ((2, 4, 4, 5, 80, 128), BF),
    ((2, 4, 4, 4, 80, 128), BF),
    ((4, 64, 128), BF),
    ((2, 4, 64, 128), BF),
    ((4, 4, 2, 640), F32),
    ((4, 4, 8, 256), F32),
    ((4, 4, 8, 256), F32),
    ((4, 8, 256), F32),
    ((4, 8, 256), F32),
    ((2, 8, 256), F32),
    ((4, 4, 8, 256), F32),
    ((2560, 640), BF),
    ((2560, 640), BF),
    ((384, 512), F32),
    ((256, 128), F32),
    ((2, 640, 128), BF),
    ((2, 144, 640), BF),
    ((4, 128, 256), BF),
    ((3, 2, 64, 128), BF),
    ((2, 4, 4, 64, 128), BF),
    ((4, 128, 152), F32),
    ((4, 152, 128), BF),
    ((4, 2, 8, 128), F32),
    ((4, 64, 128), F32),
    ((4, 64, 128), BF),
]


def per_device(hidden_img, hidden_txt, text_len, step_index, latent, cond, mod_weight, qkv_weight,
               kv_text_weight, q_gain, k_gain, out_weight, final_weight):
    out = pl.pallas_call(
        block_kernel,
        out_shape=jax.ShapeDtypeStruct((2, 64, 512), F32),
        in_specs=[VMEM] * 10 + [SMEM, SMEM, VMEM],
        out_specs=VMEM,
        scratch_shapes=[pltpu.VMEM(s, t) for s, t in SCRATCH] + [dma(200), dma(200)],
        compiler_params=pltpu.CompilerParams(collective_id=0, has_side_effects=True, vmem_limit_bytes=60 << 20),
        name="block",
    )(hidden_img.T, hidden_txt.T, qkv_weight.transpose(1, 0, 2), kv_text_weight.transpose(1, 0, 2), out_weight,
      final_weight.T, mod_weight.transpose(1, 2, 0), cond, q_gain.reshape(1, 64), k_gain, text_len, step_index, latent.T)
    return out[0].T, out[1].T


def solution(mesh):
    in_specs = (P("row", "col"), P("row", "col"), P(), P(), P("row", None), P(None, "row"),
                P("row", None, "col"), P("row", None, "col"), P("row", None, "col"), P(), P(),
                P("row", "col"), P("row", None))
    out_specs = (P("row", None), P("row", None))
    return jax.shard_map(per_device, mesh=mesh, in_specs=in_specs, out_specs=out_specs, check_vma=False)
```

```python
import jax
import jax.numpy as jnp
from jax import lax
from jax.experimental import pallas as pl
from jax.experimental.pallas import tpu as pltpu
from jax.sharding import PartitionSpec as P

STEPS = 28
EPS_NORM = 1e-06
WIDTH = 2432
MESH = pl.DeviceIdType.MESH
BF = jnp.bfloat16
F32 = jnp.float32
VMEM = pl.BlockSpec(memory_space=pltpu.VMEM)
SMEM = pl.BlockSpec(memory_space=pltpu.SMEM)


def place():
    r, c = lax.axis_index("row"), lax.axis_index("col")
    return r // 8, (r // 2) % 4, r % 2, c // 4, c % 4


def device(x, zl, core, y, zh):
    return ((x * 4 + zl) * 2 + core, y * 4 + zh)


def up(v, d, n=4):
    return lax.rem(v + d + n, n)


def sigma_of(step_now):
    remain = 1.0 - step_now.astype(F32) / STEPS
    return 3.0 * remain / (1.0 + 2.0 * remain)


class Post:
    def __init__(self, send_sem, recv_sem):
        self.send_sem, self.recv_sem, self.n, self.sent, self.todo = send_sem, recv_sem, 0, [], []

    def send(self, src, dst, to, got):
        k = self.n
        self.n += 1
        copy = pltpu.make_async_remote_copy(
            src_ref=src, dst_ref=dst, send_sem=self.send_sem.at[k], recv_sem=self.recv_sem.at[k],
            device_id=to, device_id_type=MESH)
        copy.start()
        self.sent.append(copy)
        back = pltpu.make_async_remote_copy(
            src_ref=got, dst_ref=got, send_sem=self.send_sem.at[k], recv_sem=self.recv_sem.at[k],
            device_id=to, device_id_type=MESH)
        todo = [True]
        self.todo.append((todo, back.wait_recv))

        def wait():
            assert todo[0]
            todo[0] = False
            back.wait_recv()
        return wait

    def finish(self):
        for copy in self.sent:
            copy.wait_send()


def drain(post):
    for todo, wait in post.todo:
        if todo[0]:
            wait()
    post.finish()


def tdot(a, b):
    return lax.dot_general(a, b, (((0,), (0,)), ((), ())), preferred_element_type=F32)


def all_of(waits):
    for wait in waits:
        wait()


def block_kernel(h_in, t_in, qkv_in, kv_in, ow_in, fw_in, mw_in, cond, qg, kg, text_len, step_index, latent,
                 out, X, W, OW, FX, FW, SS, mp, mx, ms, ml, tot, M, W2, R, PI, PT, KB, VB, QC, AT, A, acc, U, ST, VP, VZ,
                 send_sem, recv_sem):
    x, zl, core, y, zh = place()
    me = x * 4 + zl

    def at_x(d):
        return device(up(x, d), zl, core, y, zh)

    def at_y(d):
        return device(x, zl, core, up(y, d), zh)

    def at_zh(d):
        return device(x, zl, core, y, up(zh, d))

    def at_zl(d):
        return device(x, up(zl, d), core, y, zh)

    partner = device(x, zl, 1 - core, y, zh)
    three = (1, 3, 2)
    peers = [f(d) for f in (at_x, at_y, at_zl) for d in three] + [at_zh(1), at_zh(-1), partner]
    barrier = pltpu.get_barrier_semaphore()
    for p in peers:
        pl.semaphore_signal(barrier, inc=1, device_id=p, device_id_type=MESH)

    own = jnp.concatenate([h_in[...], jnp.concatenate([t_in[...], jnp.zeros((152, 32), BF)], axis=1)], axis=1)
    X[y, zh] = own
    v = own.astype(F32)
    SS[y, zh] = jnp.concatenate([jnp.sum(v, axis=0, keepdims=True), jnp.sum(v * v, axis=0, keepdims=True)], axis=0)
    W[core, x, zl] = jnp.zeros((5, 80, 128), BF)
    W[core, x, zl, 0:3, 0:76] = qkv_in[...]
    W[core, x, zl, 3, 0:76] = kv_in[:, 0]
    W[core, x, zl, 4, 0:76] = kv_in[:, 1]
    FX[x] = jnp.concatenate([fw_in[...], jnp.zeros((64, 52), BF)], axis=1)
    o = ow_in[...]
    OW[core, x, zl, zh, 0:64] = o[:, :128]
    OW[core, x, zl, zh, 64:80] = jnp.concatenate(
        [o[16 * g:16 * g + 16, 128:152] for g in range(4)] + [jnp.zeros((16, 32), BF)], axis=1)
    mp[...] = jnp.zeros_like(mp)
    pl.semaphore_wait(barrier, len(peers))

    post = Post(send_sem, recv_sem)
    send = post.send
    lo, hi = pl.ds(0, 80), pl.ds(80, 72)

    def relay(a, to, got):
        return send(a, a, to, got)

    LO, HI = [(0, 80)], [(80, 72)]

    class Rows:
        def __init__(self, z):
            self.z, self.low, self.high, self.rest = z, [], [], []

        def out(self, chunks):
            for first, size in chunks:
                ch = pl.ds(first, size)
                a = X.at[y, self.z, ch]
                got = (relay(a, at_y(1), X.at[up(y, -1), self.z, ch]), relay(a, at_y(-1), X.at[up(y, 1), self.z, ch]))
                if first < 80:
                    self.low.append((got[0], ch))
                    self.rest.append(got[1])
                else:
                    self.high.append((got[1], ch))
                    self.rest.append(got[0])

        def on(self, which):
            for wait, ch in which:
                e = -1 if which is self.low else 1
                wait()
                a = X.at[up(y, e), self.z, ch]
                self.rest.append(relay(a, at_y(-e), X.at[up(y, 2), self.z, ch]))

        def done(self):
            all_of(self.rest)

    def along_z(buf, first=None):
        a = buf(zh)
        return relay(a, at_zh(1), buf(up(zh, -1))), relay(a, at_zh(-1), buf(up(zh, 1)))

    def on_z(buf, waits):
        all_of(waits)
        return relay(buf(up(zh, -1)), at_zh(1), buf(up(zh, 2)))

    def x_out(part):
        a = part(x)
        return relay(a, at_x(1), part(up(x, -1))), relay(a, at_x(-1), part(up(x, 1)))

    def x_on(part, waits, n):
        waits[0]()
        t, u = pl.ds(0, n[0]), pl.ds(n[0], n[1])
        f = relay(part(up(x, -1)).at[t], at_x(1), part(up(x, 2)).at[t])
        waits[1]()
        g = relay(part(up(x, 1)).at[u], at_x(-1), part(up(x, 2)).at[u])
        return f, g

    def w_part(d):
        return lambda i: W.at[core, i, up(zl, d)]

    def across(ref, d):
        return relay(ref.at[core, :, up(zl, d)], partner, ref.at[1 - core, :, up(zl, d)])

    rows = [Rows(zh), Rows(up(zh, -1)), Rows(up(zh, 1)), Rows(up(zh, 2))]
    ss_z = along_z(lambda z: SS.at[y, z])
    w_x0 = x_out(w_part(0))
    rows[0].out(LO + HI)
    C0, C1, C2, C3 = (0, 48), (48, 32), (80, 48), (128, 24)

    def z_up(c):
        ch = pl.ds(*c)
        return relay(X.at[y, zh, ch], at_zh(1), X.at[y, up(zh, -1), ch])

    def z_down(c):
        ch = pl.ds(*c)
        return relay(X.at[y, zh, ch], at_zh(-1), X.at[y, up(zh, 1), ch])

    def w_to(d):
        return relay(W.at[core, x, zl], at_zl(d), W.at[core, x, up(zl, -d)])

    zp_0, zm_2 = z_up(C0), z_down(C2)

    c = cond[...]
    act = (c * jax.nn.sigmoid(c)).astype(BF)
    for g in range(7):
        t = lax.dot_general(act, mw_in[g], (((1,), (1,)), ((), ())), preferred_element_type=F32)
        for i in range(4):
            mp[i, :, g, 0:152] = t[4 * i:4 * i + 4]
    mods = [send(mp.at[up(x, d)], mx.at[x], at_x(d), mx.at[up(x, -d)]) for d in three]
    f_x = [relay(FX.at[x], at_x(d), FX.at[up(x, -d)]) for d in three]
    mx[x] = mp[x]
    all_of(mods)
    ms[...] = (mx[0] + mx[1]) + (mx[2] + mx[3])
    mods = [send(ms.at[up(zl, d)], ml.at[zl], at_zl(d), ml.at[up(zl, -d)]) for d in three]
    zp_1, zm_3 = z_up(C1), z_down(C3)
    ml[zl] = ms[zl]
    w_x0 = x_on(w_part(0), w_x0, (3, 2))
    ss_f = on_z(lambda z: SS.at[y, z], ss_z)
    rows[0].on(rows[0].low)
    rows[0].on(rows[0].high)
    all_of(mods)
    tot[core] = (ml[0] + ml[1]) + (ml[2] + ml[3])
    tw = relay(tot.at[core], partner, tot.at[1 - core])
    tw()
    M[y, zh] = tot[0] + tot[1]
    m_z = along_z(lambda z: M.at[y, z])
    w_z = [w_to(1), w_to(3)]
    ss_f()
    ss_y = [relay(SS.at[y], at_y(d), SS.at[up(y, -d)]) for d in three]
    all_of(w_x0)
    w_a = [across(W, 0)]
    m_f = on_z(lambda z: M.at[y, z], m_z)
    w_z.append(w_to(2))
    zp_2, zm_1 = z_up(C2), z_down(C1)
    w_z[0]()
    w_x3 = x_out(w_part(-1))
    w_z[1]()
    w_x1 = x_out(w_part(1))
    zp_0()
    rows[1].out([C0])
    zm_2()
    rows[2].out([C2])
    zp_3, zm_0 = z_up(C3), z_down(C0)
    m_f()
    m_y = [relay(M.at[y], at_y(d), M.at[up(y, -d)]) for d in three]
    w_x3 = x_on(w_part(-1), w_x3, (3, 2))
    w_x1 = x_on(w_part(1), w_x1, (3, 2))
    all_of(f_x)
    FW[core, zl] = FX[y]
    zp_1()
    rows[1].out([C1])
    zm_3()
    rows[2].out([C3])
    zpf = []
    for c in (C0, C1):
        ch = pl.ds(*c)
        zpf.append(relay(X.at[y, up(zh, -1), ch], at_zh(1), X.at[y, up(zh, 2), ch]))
    for c in (C2, C3):
        ch = pl.ds(*c)
        zpf.append(relay(X.at[y, up(zh, 1), ch], at_zh(-1), X.at[y, up(zh, 2), ch]))
    w_z[2]()
    w_x2 = x_out(w_part(2))
    all_of(ss_y)
    s = jnp.zeros((2, 640), F32)
    for i in range(16):
        s = s + SS[i // 4, i % 4]
    s = s / WIDTH
    mean = s[0:1]
    rs = lax.rsqrt(s[1:2] - mean * mean + EPS_NORM)
    o_h = along_z(lambda z: OW.at[core, x, zl, z])
    all_of(w_x3)
    w_a.append(across(W, -1))
    all_of(w_x1)
    w_a.append(across(W, 1))
    w_x2 = x_on(w_part(2), w_x2, (3, 2))
    zp_2()
    rows[1].out([C2])
    zm_1()
    rows[2].out([C1])
    rows[1].on(rows[1].low)
    rows[2].on(rows[2].high)
    rows[0].done()
    zp_3()
    rows[1].out([C3])
    zm_0()
    rows[2].out([C0])
    f_z = [relay(FW.at[core, zl], at_zl(d), FW.at[core, up(zl, -d)]) for d in three]
    all_of(w_x2)
    w_a.append(across(W, 2))
    o_hf = on_z(lambda z: OW.at[core, x, zl, z], o_h)
    all_of(w_a)

    def join(i, carry):
        xx, ll = lax.rem(i, 4), up(zh, i // 4)
        for g in range(5):
            a = W[0, xx, ll, g].astype(F32)
            b = W[1, xx, ll, g].astype(F32)
            w = jnp.concatenate([a[:76], b[:76], jnp.zeros((8, 128), F32)], axis=0)
            W2[pl.ds(pl.multiple_of(160 * i, 32), 160), 128 * g:128 * g + 128] = w.astype(BF)
        return carry

    lax.fori_loop(0, 16, join, 0)
    rows[1].on(rows[1].high)
    rows[2].on(rows[2].low)
    o_hf()
    o_l = [relay(OW.at[core, x, zl], at_zl(d), OW.at[core, x, up(zl, -d)]) for d in three]

    def ready(k):
        def one(i, carry):
            yy, zz = i, up(zh, k)
            v = (X[yy, zz].astype(F32) - mean) * rs
            m = M[yy, zz].T
            a = v[:, :512] * (1.0 + m[:152, 1:2]) + m[:152, 0:1]
            b = v[:, 512:] * (1.0 + m[:152, 4:5]) + m[:152, 3:4]
            r = jnp.concatenate([jnp.concatenate([a, b], axis=1), jnp.zeros((8, 640), F32)], axis=0)
            R[pl.ds(pl.multiple_of(640 * k + 160 * i, 32), 160)] = r.astype(BF)
            return carry

        lax.fori_loop(0, 4, one, 0)

    def dots(k, a, b, image):
        n = 640 * k
        lanes = slice(0, 512) if image else slice(512, 640)
        return tdot(W2[n:n + 640, a:b], R[n:n + 640, lanes])

    def o_part(d):
        return lambda i: OW.at[core, i, up(zl, d)]

    def background():
        def fan(d):
            part = o_part(d)
            return [relay(part(x), at_x(e), part(up(x, -e))) for e in three]

        x0 = fan(0)
        yield
        o_l[0]()
        x3 = fan(-1)
        o_l[1]()
        x1 = fan(1)
        yield
        o_l[2]()
        x2 = fan(2)
        all_of(x0)
        last = [across(OW, 0)]
        yield
        yield
        all_of(x3)
        last.append(across(OW, -1))
        all_of(x1)
        last.append(across(OW, 1))
        yield
        yield
        all_of(x2)
        last.append(across(OW, 2))
        all_of(last)
        yield

    def add(k):
        ready(k)
        PI[...] += dots(k, 0, 384, True)
        PT[...] += dots(k, 384, 640, False)

    work = background()
    all_of(m_y)
    ready(0)
    PI[...] = dots(0, 0, 384, True)
    PT[...] = dots(0, 384, 640, False)
    zpf[0]()
    rows[3].out([C0])
    zpf[2]()
    rows[3].out([C2])
    next(work, None)
    rows[1].done()
    add(3)
    zpf[1]()
    rows[3].out([C1])
    zpf[3]()
    rows[3].out([C3])
    rows[2].done()
    add(1)
    rows[3].on(rows[3].low)
    rows[3].on(rows[3].high)
    all_of(f_z)
    f_a = [relay(FW.at[core], partner, FW.at[1 - core])]
    next(work, None)
    rows[3].done()
    ready(2)

    def normed(u, g):
        square = jnp.mean(u * u, axis=0, keepdims=True)
        return u * lax.rsqrt(square + EPS_NORM) * g

    def two(u, g):
        return jnp.concatenate([normed(u[:64], g), normed(u[64:], g)], axis=0)

    G = jnp.concatenate([qg[...], kg[...], jnp.zeros((5, 64), F32)], axis=0)
    G = jnp.concatenate([G, G], axis=1).T[:64]
    kv = PI[128:384] + dots(2, 128, 384, True)
    tkv = PT[...] + dots(2, 384, 640, False)
    KB[0, :512] = two(kv[:128], G[:, 1:2]).T.astype(BF)
    KB[0, 512:] = two(tkv[:128], G[:, 2:3]).T.astype(BF)
    VB[0, :128, :512] = kv[128:].astype(BF)
    VB[0, :128, 512:] = tkv[128:].astype(BF)
    VB[0, 128:] = jnp.ones((16, 640), BF)
    waits = [send(KB.at[0], KB.at[1], partner, KB.at[1]), send(VB.at[0], VB.at[1], partner, VB.at[1])]
    qt = two(PI[0:128] + dots(2, 0, 128, True), G[:, 0:1])
    head = lax.broadcasted_iota(jnp.int32, (128, 512), 0) // 64
    qz = [jnp.where(head == h, qt, 0.0).astype(BF) * 0.125 for h in range(2)]
    for t in range(4):
        QC[t] = jnp.concatenate([qz[0][:, 128 * t:128 * t + 128], qz[1][:, 128 * t:128 * t + 128]], axis=1)
    next(work, None)
    all_of(waits)

    length = text_len[me]
    slot = lax.broadcasted_iota(jnp.int32, (128, 256), 0)
    valid = [(slot < 96) & (slot + 96 * owner < length) for owner in (core, 1 - core)]
    a_z = {}
    for d in (2, 1, 3, 0):
        t = QC[up(zh, d)]
        scores = []
        for j in range(2):
            sc = jnp.dot(KB[j], t, preferred_element_type=F32)
            scores += [sc[:512], jnp.where(valid[j], sc[512:], -jnp.inf)]
        top = scores[0].max(axis=0, keepdims=True)
        for sc in scores[1:]:
            top = jnp.maximum(top, sc.max(axis=0, keepdims=True))
        p = [jnp.exp(sc - top).astype(BF) for sc in scores]
        o = 0.0
        for j in range(2):
            o = o + jnp.dot(VB[j, :, :512], p[2 * j], preferred_element_type=F32)
            o = o + jnp.dot(VB[j, :, 512:], p[2 * j + 1], preferred_element_type=F32)
        o = o[:128] / o[128:129]
        if d:
            AT[d - 1, 0] = o[:64, :128].astype(BF)
            AT[d - 1, 1] = o[64:, 128:].astype(BF)
            a_z[d] = send(AT.at[d - 1], A.at[:, y, zh], at_zh(d), A.at[:, y, up(zh, -d)])
        else:
            A[0, y, zh] = o[:64, :128].astype(BF)
            A[1, y, zh] = o[64:, 128:].astype(BF)
        next(work, None)

    a_y = []

    def along_y(z):
        for e in (1, 3, 2):
            a_y.append(relay(A.at[:, y, z], at_y(e), A.at[:, up(y, -e), z]))

    along_y(zh)
    for d in (1, 3, 2):
        a_z[d]()
        along_y(up(zh, -d))
    all_of(f_a)
    fw = [jnp.concatenate([FW[0, z][:, :76], FW[1, z][:, :76]], axis=1) for z in range(4)]
    for _ in work:
        pass

    def project(yy, first):
        for z in range(4):
            t = 0.0
            for h in range(2):
                a = A[h, yy].reshape(256, 128)
                w = OW[h, yy, :, z]
                tail = jnp.concatenate([w[:, 64:80, 24 * g:24 * g + 24] for g in range(4)], axis=1)
                w = jnp.concatenate([w[:, :64], tail], axis=2).reshape(256, 152)
                t = t + tdot(a, w)
            acc[z] = t if first else acc[z] + t

    project(y, True)
    for k, e in enumerate((1, 3, 2)):
        all_of(a_y[k::3])
        project(up(y, -e), False)
    s = q = jnp.zeros((8, 128), F32)
    mine = pl.ds(pl.multiple_of(128 * zh, 128), 128)
    for z in range(4):
        m = M[y, z].T
        u = (X[y, z, :, mine].astype(F32) + m[:152, 2:3] * acc[z].T).astype(BF)
        U[z] = u
        v = u.astype(F32)
        s = s + v.reshape(19, 8, 128).sum(axis=0)
        q = q + (v * v).reshape(19, 8, 128).sum(axis=0)
    ST[y, 0] = s
    ST[y, 1] = q
    all_of([relay(ST.at[y], at_y(d), ST.at[up(y, -d)]) for d in (1, 3, 2)])
    st = ST[0] + ST[1] + (ST[2] + ST[3])
    mean = jnp.sum(st[0], axis=0, keepdims=True) / WIDTH
    square = jnp.sum(st[1], axis=0, keepdims=True) / WIDTH
    rs = lax.rsqrt(square - mean * mean + EPS_NORM)
    vel = 0.0
    for z in range(4):
        m = M[y, z].T
        head_in = ((U[z].astype(F32) - mean) * rs) * (1.0 + m[:152, 6:7]) + m[:152, 5:6]
        vel = vel + jnp.dot(fw[z], head_in.astype(BF), preferred_element_type=F32)
    VP[y] = vel
    all_of([relay(VP.at[y], at_y(d), VP.at[up(y, -d)]) for d in (1, 3, 2)])
    VZ[zh] = (VP[0] + VP[1] + (VP[2] + VP[3])).astype(BF)
    all_of([relay(VZ.at[zh], at_zh(d), VZ.at[up(zh, -d)]) for d in (2, 1, 3)])
    now = jnp.full((8, 128), step_index[me], jnp.int32)
    step = (sigma_of(now + 1) - sigma_of(now))[0:1]
    for z in range(4):
        v = VZ[z].astype(F32)
        out[0, :, 128 * z:128 * z + 128] = v
        out[1, :, 128 * z:128 * z + 128] = latent[:, 128 * z:128 * z + 128] + step * v
    post.finish()


def dma(n):
    return pltpu.SemaphoreType.DMA((n,))


SCRATCH = [
    ((4, 4, 152, 640), BF),
    ((2, 4, 4, 5, 80, 128), BF),
    ((2, 4, 4, 4, 80, 128), BF),
    ((4, 64, 128), BF),
    ((2, 4, 64, 128), BF),
    ((4, 4, 2, 640), F32),
    ((4, 4, 8, 256), F32),
    ((4, 4, 8, 256), F32),
    ((4, 8, 256), F32),
    ((4, 8, 256), F32),
    ((2, 8, 256), F32),
    ((4, 4, 8, 256), F32),
    ((2560, 640), BF),
    ((2560, 640), BF),
    ((384, 512), F32),
    ((256, 128), F32),
    ((2, 640, 128), BF),
    ((2, 144, 640), BF),
    ((4, 128, 256), BF),
    ((3, 2, 64, 128), BF),
    ((2, 4, 4, 64, 128), BF),
    ((4, 128, 152), F32),
    ((4, 152, 128), BF),
    ((4, 2, 8, 128), F32),
    ((4, 64, 128), F32),
    ((4, 64, 128), BF),
]


def per_device(hidden_img, hidden_txt, text_len, step_index, latent, cond, mod_weight, qkv_weight,
               kv_text_weight, q_gain, k_gain, out_weight, final_weight):
    out = pl.pallas_call(
        block_kernel,
        out_shape=jax.ShapeDtypeStruct((2, 64, 512), F32),
        in_specs=[VMEM] * 10 + [SMEM, SMEM, VMEM],
        out_specs=VMEM,
        scratch_shapes=[pltpu.VMEM(s, t) for s, t in SCRATCH] + [dma(200), dma(200)],
        compiler_params=pltpu.CompilerParams(collective_id=0, has_side_effects=True, vmem_limit_bytes=60 << 20),
        name="block",
    )(hidden_img.T, hidden_txt.T, qkv_weight.transpose(1, 0, 2), kv_text_weight, out_weight,
      final_weight.T, mod_weight.transpose(1, 2, 0), cond, q_gain.reshape(1, 64), k_gain, text_len, step_index, latent.T)
    return out[0].T, out[1].T


def solution(mesh):
    in_specs = (P("row", "col"), P("row", "col"), P(), P(), P("row", None), P(None, "row"),
                P("row", None, "col"), P("row", None, "col"), P("row", None, "col"), P(), P(),
                P("row", "col"), P("row", None))
    out_specs = (P("row", None), P("row", None))
    return jax.shard_map(per_device, mesh=mesh, in_specs=in_specs, out_specs=out_specs, check_vma=False)
```
